128 devices in a mesh: sky: 4 (over x), exp: 32 (over z, y, core).
Axes of the slice: x: 4, y: 4, z: 4, core: 2. Of those that a mesh axis runs over, the one named last changes fastest.
Arguments:
- obs_weight: float32 [4, 32, 32, 1024], P('sky', 'exp'), may hold values from 0.25 to 4
- magnitude: float32 [4, 32, 32, 1024], P('sky', 'exp'), may hold values from -18 to 18
- star_id: int32 [4, 32, 32, 1024], P('sky', 'exp'), may hold values from 0 to 4095
- peer_count: int32 [4, 32, 32], P('sky', 'exp'), may hold values from 1 to 1024, 24576 in all within a row
- zp_index: int32 [4, 32, 32, 1024], P('sky', 'exp'), may hold values from 0 to 12095
Outputs:
- zero_points: float32 [387072], P('exp')
- residual: float32 [387072], P('exp')
The draws below stay inside these ranges and needn't reach their ends.
Inputs may be any that keep to these rules, and one draw needn't show every extreme that they name: `peer_count`: each device's counts over the 32 owners sum to 24576, and one of them equals 1024.
All inputs are finite; a program needn't handle non-finite values.
Results may differ from the reference program's by a relative error of at most 0.0003.
Values sent between devices are 32-bit elements; how exact they have to be, the bound alone decides.
A program may use at most 64 MiB of HBM per device.

```python
import math
import jax
import jax.numpy as jnp
import numpy as np

CAP = 1024
STAR_DEV = 4096
ITERS = 2
ZP_DEV = 12096
N_SKY = 4
N_EXP = 32


def touch_ends(array, rng, smallest, high):
    longest = array.shape.index(max(array.shape))
    spots = []
    for shift in (0, 1):
        where = [jax.random.randint(jax.random.fold_in(rng, axis), (), 0, length) for axis, length in enumerate(array.shape)]
        where[longest] = (where[longest] + shift) % array.shape[longest]
        spots.append(tuple(where))
    return array.at[spots[0]].set(smallest).at[spots[1]].set(high)


def level_of(stream_key, dims, pieces, least, largest):
    def one(position, shards_of):
        steps = jax.random.uniform(jax.random.fold_in(jax.random.fold_in(stream_key, 6), position), (shards_of,), jnp.float32, least / len(pieces), largest / len(pieces))
        return jnp.repeat(jnp.exp(steps), dims[position] // shards_of).reshape((-1,) + (1,) * (len(dims) - position - 1))

    level = one(*pieces[0])
    for cut in pieces[1:]:
        level = level * one(*cut)
    return level


def profile(amount, total, limit, slope):
    loads = [(1 << 20) // math.isqrt(standing ** slope) + 1 for standing in range(2, amount + 1)]
    surplus, holding = total - limit - (amount - 1), [1] * (amount - 1)
    while surplus > 0:
        candidates = [i for i in range(amount - 1) if holding[i] < limit]
        mass, remaining = sum([loads[i] for i in candidates]), surplus
        for i in candidates:
            extra = min(limit - holding[i], max(1, remaining * loads[i] // mass), surplus)
            holding[i] = holding[i] + extra
            surplus = surplus - extra
    return np.array([limit] + holding)


def uneven_parts(stream_key, number_of, total, reach, lean):
    if number_of == 2:
        one = jax.random.randint(stream_key, (), max(1, total - reach), min(reach, total - 1) + 1)
        return jnp.stack([one, total - one])
    tallies = jnp.asarray(profile(number_of, total, reach, lean), jnp.int32)
    couples = (number_of - 1) // 2
    donor, taker = tallies[1:1 + 2 * couples:2], tallies[2:2 + 2 * couples:2]
    slack = jnp.minimum(donor - 1, reach - taker)
    shifted = jax.random.randint(jax.random.fold_in(stream_key, 1), (couples,), 0, 1 << 20) % (slack + 1)
    tallies = tallies.at[1:1 + 2 * couples:2].set(donor - shifted).at[2:2 + 2 * couples:2].set(taker + shifted)
    return tallies[jax.random.permutation(jax.random.fold_in(stream_key, 2), number_of)]


def noise(key, extent, deviation, most, cuts=(), held_as=jnp.bfloat16):
    result = deviation * jax.random.normal(key, extent, jnp.float32)
    if cuts:
        result = result * level_of(key, extent, cuts, -0.22, 0.18)
    return jnp.clip(result, -most, most).astype(held_as)


def setup_inputs(seed: int = 0) -> dict:
    seeds = jax.random.split(jax.random.key(seed), 6)
    obs_weight = jnp.clip(jnp.exp(math.log(4.0) - 2.7725887 * jax.random.uniform(seeds[0], (N_SKY, N_EXP, N_EXP, CAP), jnp.float32) ** level_of(seeds[0], (N_SKY, N_EXP, N_EXP, CAP), ((0, 4), (1, 32)), -0.2, 0.2)), 0.25, 4.0)
    magnitude = noise(seeds[1], (N_SKY, N_EXP, N_EXP, CAP), 3.0, 18.0, ((0, 4), (1, 32)), jnp.float32)
    star_id = touch_ends(jax.random.randint(seeds[2], (N_SKY, N_EXP, N_EXP, CAP), 0, STAR_DEV), jax.random.fold_in(seeds[2], 1), 0, STAR_DEV - 1).astype(jnp.int32)
    peer_count = jax.vmap(lambda own: uneven_parts(own, N_EXP, N_EXP * CAP * 3 // 4, CAP, 2))(jax.random.split(seeds[3], N_SKY * N_EXP)).reshape((N_SKY, N_EXP, N_EXP)).astype(jnp.int32)
    zp_index = touch_ends(jax.random.randint(seeds[4], (N_SKY, N_EXP, N_EXP, CAP), 0, ZP_DEV), jax.random.fold_in(seeds[4], 1), 0, ZP_DEV - 1).astype(jnp.int32)
    return dict(obs_weight=obs_weight, magnitude=magnitude, star_id=star_id, peer_count=peer_count, zp_index=zp_index)


ridge = 1.0
prior = 1.0


def reference(obs_weight, magnitude, star_id, peer_count, zp_index):
    n_sky = obs_weight.shape[0]
    n_exp = obs_weight.shape[1]
    slots = jnp.arange(CAP, dtype=jnp.int32)
    live = (slots[None, None, None, :] < peer_count[..., None]).astype(jnp.float32)
    weight = obs_weight * live
    device = (jnp.arange(n_sky, dtype=jnp.int32)[:, None] * n_exp + jnp.arange(n_exp, dtype=jnp.int32)[None, :])
    segment = (device[:, :, None, None] * STAR_DEV + star_id).reshape(-1)
    nstars = n_sky * n_exp * STAR_DEV
    wsum = prior + jax.ops.segment_sum(weight.reshape(-1), segment, nstars)
    owner = jnp.arange(n_exp, dtype=jnp.int32)[None, None, :, None]
    target = (owner * ZP_DEV + jnp.transpose(zp_index, (0, 2, 1, 3))).reshape(-1)
    flat_w = weight.reshape(-1)

    def reduce_slots(values):
        flat = values.reshape(-1)
        mean = jax.ops.segment_sum(flat_w * flat, segment, nstars) / wsum
        term = flat_w * (flat - mean[segment])
        return jax.ops.segment_sum(term, target, n_exp * ZP_DEV)

    def operate(field):
        return reduce_slots(field[target]) + ridge * field

    right = reduce_slots(magnitude)
    zero_points = jnp.zeros_like(right)
    residual = right
    direction = right
    norm_now = jnp.sum(residual * residual)
    for step in range(ITERS):
        image = operate(direction)
        alpha = norm_now / jnp.sum(direction * image)
        zero_points = zero_points + alpha * direction
        residual = residual - alpha * image
        norm_next = jnp.sum(residual * residual)
        direction = residual + (norm_next / norm_now) * direction
        norm_now = norm_next
    return zero_points, residual
```

```python
import functools

import jax
import jax.numpy as jnp
from jax import lax
from jax.experimental import pallas as pl
from jax.experimental.pallas import tpu as pltpu
from jax.sharding import PartitionSpec as P

CAP = 1024
STAR_DEV = 4096
ZP_DEV = 12096
LANES = 128
SUB = CAP // LANES
STAR_ROWS = STAR_DEV // LANES
ZP_ROWS = (ZP_DEV + LANES - 1) // LANES
ZP_PAD = 96
PLANE = 8

ridge = 1.0
prior = 1.0
f32 = jnp.float32
bf16 = jnp.bfloat16
NT = (((1,), (1,)), ((), ()))
MESH = pl.DeviceIdType.MESH


def two_parts(x):
    coarse = x.astype(bf16)
    return coarse, (x - coarse.astype(f32)).astype(bf16)


def as_code(x):
    return x.astype(f32).astype(bf16)


def row_of(x, r, n):
    return jnp.broadcast_to(x[r : r + 1, :], (n, LANES))


def scatter(high, low, parts, n_high, n_low):
    rows = high.shape[0]
    iota_high = as_code(lax.broadcasted_iota(jnp.int32, (n_high, LANES), 0))
    iota_low = as_code(lax.broadcasted_iota(jnp.int32, (n_low, LANES), 0))
    one, zero = jnp.ones((), bf16), jnp.zeros((), bf16)
    hot, weighted = [], [[] for _ in parts]
    for r in range(rows):
        hot.append(jnp.where(row_of(high, r, n_high) == iota_high, one, zero))
        mask = row_of(low, r, n_low) == iota_low
        for column, part in zip(weighted, parts):
            column.append(jnp.where(mask, row_of(part, r, n_low), zero))
    hot = jnp.concatenate(hot, axis=1)
    weighted = jnp.concatenate([jnp.concatenate(c, axis=1) for c in weighted], axis=0)
    return lax.dot_general(hot, weighted, NT, preferred_element_type=f32)


def pick(table, rows, index):
    high, low = lax.shift_right_logical(index, 7), index & 127
    found = jnp.zeros(index.shape, f32)
    for r in range(rows):
        line = jnp.broadcast_to(table[r : r + 1, :], index.shape)
        found = jnp.where(high == r, jnp.take_along_axis(line, low, axis=1), found)
    return found


def star_codes(index):
    high = lax.shift_right_logical(index, 7) + STAR_ROWS * (lax.shift_right_logical(index, 5) & 3)
    return as_code(high), as_code(index & 31)


def zp_codes(index):
    high = lax.shift_right_logical(index, 7) + ZP_PAD * (lax.shift_right_logical(index, 6) & 1)
    return as_code(high), as_code(index & 63)


def star_table(pair):
    both = pair[:, :32] + pair[:, 32:64]
    return jnp.concatenate([both[32 * q : 32 * q + 32, :] for q in range(4)], axis=1)


def kernel(
    n_sky, n_exp,
    count, weight_in, magnitude_in, star_in, zp_in,
    x_out, r_out,
    weight, magnitude, star, zp, wsum, mean, field, image, image2,
    sent, got, shares, dots, loads, sends, arrivals,
):
    sky, me = lax.axis_index("sky"), lax.axis_index("exp")
    my_z, my_y, my_c = me // 8, (me // 2) % 4, me % 2
    planes = n_exp // PLANE

    incoming = []
    for a, (source, target) in enumerate(((weight_in, weight), (magnitude_in, magnitude), (star_in, star), (zp_in, zp))):
        for c in range(SUB):
            copy = pltpu.make_async_copy(
                source.at[0, 0, :, pl.ds(c * LANES, LANES)], target.at[:, c, :], loads.at[a, c])
            copy.start()
            incoming.append(copy)

    barrier = pltpu.get_barrier_semaphore()

    @pl.loop(1, n_exp)
    def _(t):
        pl.semaphore_signal(barrier, inc=1, device_id={"exp": lax.rem(me + t, n_exp)}, device_id_type=MESH)

    for t in range(1, n_sky):
        pl.semaphore_signal(barrier, inc=1, device_id={"sky": lax.rem(sky + t, n_sky)}, device_id_type=MESH)

    for copy in incoming:
        copy.wait()

    slot = lax.broadcasted_iota(jnp.int32, (SUB, LANES), 0) * LANES + lax.broadcasted_iota(jnp.int32, (SUB, LANES), 1)

    @pl.loop(0, n_exp)
    def _(j):
        weight[j] = jnp.where(slot < count[0, 0, j], weight[j], 0.0)

    def flat(x):
        return x.reshape(PLANE * SUB, LANES)

    def plane(ref, base):
        return flat(ref[pl.ds(base, PLANE)])

    def first(g, total):
        base = pl.multiple_of(g * PLANE, PLANE)
        w = plane(weight, base)
        high, low = star_codes(plane(star, base))
        return total + scatter(high, low, two_parts(w) + two_parts(w * plane(magnitude, base)), 128, 32)

    total = lax.fori_loop(0, planes, first, jnp.zeros((128, 128), f32))
    wsum[...] = prior + star_table(total[:, :64])
    mean[...] = star_table(total[:, 64:]) / wsum[...]

    pl.semaphore_wait(barrier, n_exp - 1 + n_sky - 1)

    def exchange(phase, block):
        def send(j, step):
            pltpu.make_async_remote_copy(
                src_ref=sent.at[phase, j], dst_ref=got.at[phase, me],
                send_sem=sends.at[phase], recv_sem=arrivals.at[phase, step],
                device_id={"exp": j}, device_id_type=MESH).start()

        def plane_of(step, last):
            z = lax.rem(my_z + (planes - 1 - step), planes)
            spots = [(dy, dc) for dy in (2, 1, 3, 0) for dc in (1, 0)]
            before = None
            for dy, dc in spots:
                j = z * 8 + lax.rem(my_y + dy, 4) * 2 + lax.rem(my_c + dc, 2)
                if last and (dy, dc) == (0, 0):
                    got[phase, me] = block(me)
                else:
                    sent[phase, j] = block(j)
                if before is not None:
                    send(before, step)
                before = None if last and (dy, dc) == (0, 0) else j
            if before is not None:
                send(before, step)

        @pl.loop(0, planes - 1)
        def _(step):
            plane_of(step, False)

        plane_of(planes - 1, True)

    def arrive(phase, step, blocks):
        pltpu.make_async_copy(
            sent.at[phase, pl.ds(0, blocks)], got.at[phase, pl.ds(0, blocks)], arrivals.at[phase, step]).wait()

    def over_planes(phase, shape, part):
        def one(step, total):
            arrive(phase, step, PLANE)
            return total + part(pl.multiple_of(lax.rem(my_z + 1 + step, planes) * PLANE, PLANE))

        total = lax.fori_loop(0, planes - 1, one, jnp.zeros(shape, f32))
        arrive(phase, planes - 1, PLANE - 1)
        return total + part(pl.multiple_of(my_z * PLANE, PLANE))

    def to_owners(phase, values):
        exchange(phase, lambda j: weight[j] * (values(j) - pick(mean, STAR_ROWS, star[j])))

    def from_owners(phase, source):
        exchange(phase, lambda k: pick(source, ZP_ROWS, zp[k]))

    def star_means(phase):
        def part(base):
            high, low = star_codes(plane(star, base))
            return scatter(high, low, two_parts(plane(weight, base) * flat(got[phase, pl.ds(base, PLANE)])), 128, 32)

        mean[...] = star_table(over_planes(phase, (128, 64), part)) / wsum[...]

    def owner_sums(phase, turn):
        def part(base):
            high, low = zp_codes(plane(zp, base))
            return scatter(high, low, two_parts(flat(got[phase, pl.ds(base, PLANE)])), 2 * ZP_PAD, 64)

        pair = over_planes(phase, (2 * ZP_PAD, 128), part)
        both = pair + pltpu.roll(pair, 64, 1)
        lane = lax.broadcasted_iota(jnp.int32, (ZP_PAD, LANES), 1)
        shares[turn, sky] = jnp.where(lane < 64, both[:ZP_PAD], both[ZP_PAD:])
        for t in (2, 1, 3):
            pltpu.make_async_remote_copy(
                src_ref=shares.at[turn, sky], dst_ref=shares.at[turn, sky],
                send_sem=sends.at[5 + turn], recv_sem=arrivals.at[5 + turn, 0],
                device_id={"sky": lax.rem(sky + t, n_sky)}, device_id_type=MESH).start()
        pltpu.make_async_copy(
            shares.at[turn, pl.ds(0, 3)], shares.at[turn, pl.ds(0, 3)], arrivals.at[5 + turn, 0]).wait()
        return (shares[turn, 0] + shares[turn, 1]) + (shares[turn, 2] + shares[turn, 3])

    def put_dots(turn, pairs):
        rows = [jnp.sum(a * b, axis=0, keepdims=True) for a, b in pairs]
        rows += [jnp.zeros((1, LANES), f32)] * (SUB - len(rows))
        dots[turn, me] = jnp.concatenate(rows, axis=0)

        @pl.loop(1, n_exp)
        def _(t):
            pltpu.make_async_remote_copy(
                src_ref=dots.at[turn, me], dst_ref=dots.at[turn, me],
                send_sem=sends.at[8 + turn], recv_sem=arrivals.at[8 + turn, 0],
                device_id={"exp": lax.rem(me + n_exp - t, n_exp)}, device_id_type=MESH).start()

    def take_dots(turn):
        pltpu.make_async_copy(
            dots.at[turn, pl.ds(0, n_exp - 1)], dots.at[turn, pl.ds(0, n_exp - 1)], arrivals.at[8 + turn, 0]).wait()
        return jnp.sum(jnp.sum(dots[turn], axis=0), axis=1, keepdims=True)

    to_owners(0, lambda j: magnitude[j])
    field[...] = owner_sums(0, 0)
    from_owners(1, field)
    star_means(1)
    to_owners(2, lambda j: got[1, j])
    image[...] = owner_sums(2, 1) + ridge * field[...]
    put_dots(0, ((field[...], field[...]), (field[...], image[...])))
    from_owners(3, image)
    star_means(3)
    to_owners(4, lambda j: got[3, j])
    image2[...] = owner_sums(4, 2) + ridge * image[...]

    def whole(x):
        return jnp.broadcast_to(jnp.broadcast_to(x, (1, LANES)), (ZP_PAD, LANES))

    b, c, d = field[...], image[...], image2[...]
    sums = take_dots(0)
    norm_now = sums[0:1]
    alpha = norm_now / sums[1:2]
    residual = b - whole(alpha) * c
    along = c - whole(alpha) * d
    put_dots(1, ((residual, residual), (residual, along), (residual, c), (b, along)))
    later = take_dots(1)
    norm_next = later[0:1]
    ratio = norm_next / norm_now
    curve = later[1:2] + ratio * (later[2:3] + later[3:4]) + ratio * ratio * sums[1:2]
    step = norm_next / curve
    x_out[...] = whole(alpha) * b + whole(step) * (residual + whole(ratio) * b)
    r_out[...] = residual - whole(step) * (along + whole(ratio) * c)

    for phase in range(5):
        pltpu.make_async_copy(
            sent.at[phase, pl.ds(0, n_exp - 1)], got.at[phase, pl.ds(0, n_exp - 1)], sends.at[phase]).wait()
    for turn in range(3):
        pltpu.make_async_copy(
            shares.at[turn, pl.ds(0, 3)], shares.at[turn, pl.ds(0, 3)], sends.at[5 + turn]).wait()
    for turn in range(2):
        pltpu.make_async_copy(
            dots.at[turn, pl.ds(0, n_exp - 1)], dots.at[turn, pl.ds(0, n_exp - 1)], sends.at[8 + turn]).wait()


def body(obs_weight, magnitude, star_id, peer_count, zp_index):
    n_sky, n_exp = lax.axis_size("sky"), lax.axis_size("exp")
    blocks = (n_exp, SUB, LANES)
    owned = jax.ShapeDtypeStruct((ZP_PAD, LANES), f32)
    anywhere = pl.BlockSpec(memory_space=pl.ANY)
    inside = pl.BlockSpec(memory_space=pltpu.VMEM)
    x, r = pl.pallas_call(
        functools.partial(kernel, n_sky, n_exp),
        out_shape=(owned, owned),
        in_specs=[pl.BlockSpec(memory_space=pltpu.SMEM)] + [anywhere] * 4,
        out_specs=(inside, inside),
        scratch_shapes=[
            pltpu.VMEM(blocks, f32),
            pltpu.VMEM(blocks, f32),
            pltpu.VMEM(blocks, jnp.int32),
            pltpu.VMEM(blocks, jnp.int32),
            pltpu.VMEM((STAR_ROWS, LANES), f32),
            pltpu.VMEM((STAR_ROWS, LANES), f32),
            pltpu.VMEM((ZP_PAD, LANES), f32),
            pltpu.VMEM((ZP_PAD, LANES), f32),
            pltpu.VMEM((ZP_PAD, LANES), f32),
            pltpu.VMEM((5,) + blocks, f32),
            pltpu.VMEM((5,) + blocks, f32),
            pltpu.VMEM((3, n_sky, ZP_PAD, LANES), f32),
            pltpu.VMEM((2, n_exp, SUB, LANES), f32),
            pltpu.SemaphoreType.DMA((4, SUB)),
            pltpu.SemaphoreType.DMA((10,)),
            pltpu.SemaphoreType.DMA((10, n_exp // PLANE)),
        ],
        compiler_params=pltpu.CompilerParams(collective_id=0, has_side_effects=True),
        name="ubercal_cg",
    )(peer_count, obs_weight, magnitude, star_id, zp_index)
    return x.reshape(-1)[:ZP_DEV], r.reshape(-1)[:ZP_DEV]


def solution(mesh):
    return jax.shard_map(
        body,
        mesh=mesh,
        in_specs=(
            P("sky", "exp", None, None),
            P("sky", "exp", None, None),
            P("sky", "exp", None, None),
            P("sky", "exp", None),
            P("sky", "exp", None, None),
        ),
        out_specs=(P("exp"), P("exp")),
        check_vma=False,
    )
```

```python
import functools

import jax
import jax.numpy as jnp
from jax import lax
from jax.experimental import pallas as pl
from jax.experimental.pallas import tpu as pltpu
from jax.sharding import PartitionSpec as P

CAP = 1024
STAR_DEV = 4096
ZP_DEV = 12096
LANES = 128
SUB = CAP // LANES
STAR_ROWS = STAR_DEV // LANES
ZP_ROWS = (ZP_DEV + LANES - 1) // LANES
ZP_PAD = 96
PLANE = 8

OFFSETS = ((0, 0), (0, 1), (0, 3), (1, 0), (3, 0), (1, 1), (0, 2), (2, 0),
           (1, 3), (3, 1), (3, 3), (2, 1), (2, 2), (2, 3), (1, 2), (3, 2))
CHIPS = len(OFFSETS)


def digits(values):
    code = sum(v << (2 * q) for q, v in enumerate(values))
    return code - (1 << 32) if code >= 1 << 31 else code


OFFSET_Z = digits([z for z, _ in OFFSETS])
OFFSET_Y = digits([y for _, y in OFFSETS])

ridge = 1.0
prior = 1.0
f32 = jnp.float32
bf16 = jnp.bfloat16
NT = (((1,), (1,)), ((), ()))
MESH = pl.DeviceIdType.MESH


def two_parts(x):
    coarse = x.astype(bf16)
    return coarse, (x - coarse.astype(f32)).astype(bf16)


def as_code(x):
    return x.astype(f32).astype(bf16)


def row_of(x, r, n):
    return jnp.broadcast_to(x[r : r + 1, :], (n, LANES))


def scatter(high, low, parts, n_high, n_low):
    rows = high.shape[0]
    iota_high = as_code(lax.broadcasted_iota(jnp.int32, (n_high, LANES), 0))
    iota_low = as_code(lax.broadcasted_iota(jnp.int32, (n_low, LANES), 0))
    one, zero = jnp.ones((), bf16), jnp.zeros((), bf16)
    hot, weighted = [], [[] for _ in parts]
    for r in range(rows):
        hot.append(jnp.where(row_of(high, r, n_high) == iota_high, one, zero))
        mask = row_of(low, r, n_low) == iota_low
        for column, part in zip(weighted, parts):
            column.append(jnp.where(mask, row_of(part, r, n_low), zero))
    hot = jnp.concatenate(hot, axis=1)
    weighted = jnp.concatenate([jnp.concatenate(c, axis=1) for c in weighted], axis=0)
    return lax.dot_general(hot, weighted, NT, preferred_element_type=f32)


def pick(table, rows, index):
    high, low = lax.shift_right_logical(index, 7), index & 127
    found = jnp.zeros(index.shape, f32)
    for r in range(rows):
        line = jnp.broadcast_to(table[r : r + 1, :], index.shape)
        found = jnp.where(high == r, jnp.take_along_axis(line, low, axis=1), found)
    return found


def star_codes(index):
    high = lax.shift_right_logical(index, 7) + STAR_ROWS * (lax.shift_right_logical(index, 5) & 3)
    return as_code(high), as_code(index & 31)


def zp_codes(index):
    high = lax.shift_right_logical(index, 7) + ZP_PAD * (lax.shift_right_logical(index, 6) & 1)
    return as_code(high), as_code(index & 63)


def star_table(pair):
    both = pair[:, :32] + pair[:, 32:64]
    return jnp.concatenate([both[32 * q : 32 * q + 32, :] for q in range(4)], axis=1)


def kernel(
    n_sky, n_exp,
    count, weight_in, magnitude_in, star_in, zp_in,
    x_out, r_out,
    weight, magnitude, star, zp, wsum, mean, fields, scale,
    sent, got, shares, dots, loads, sends, arrivals,
):
    sky, me = lax.axis_index("sky"), lax.axis_index("exp")
    my_z, my_y, my_c = me // 8, (me // 2) % 4, me % 2
    partner = 1 - my_c

    def digit(code, q):
        return lax.shift_right_logical(jnp.int32(code), 2 * q) & 3

    def member(q, sign):
        z = (my_z + 4 + sign * digit(OFFSET_Z, q)) & 3
        y = (my_y + 4 + sign * digit(OFFSET_Y, q)) & 3
        return z * 8 + y * 2

    incoming = []
    for a, (source, target) in enumerate(((weight_in, weight), (star_in, star), (magnitude_in, magnitude), (zp_in, zp))):
        for c in range(SUB):
            copy = pltpu.make_async_copy(
                source.at[0, 0, :, pl.ds(c * LANES, LANES)], target.at[:, c, :], loads.at[a, c])
            copy.start()
            incoming.append(copy)

    barrier = pltpu.get_barrier_semaphore()

    @pl.loop(1, n_exp)
    def _(t):
        pl.semaphore_signal(barrier, inc=1, device_id={"exp": lax.rem(me + t, n_exp)}, device_id_type=MESH)

    for t in range(1, n_sky):
        pl.semaphore_signal(barrier, inc=1, device_id={"sky": lax.rem(sky + t, n_sky)}, device_id_type=MESH)

    for copy in incoming[: 3 * SUB]:
        copy.wait()

    slot = lax.broadcasted_iota(jnp.int32, (SUB, LANES), 0) * LANES + lax.broadcasted_iota(jnp.int32, (SUB, LANES), 1)

    def stack(blocks):
        return jnp.concatenate(blocks, axis=0)

    def first(g, total):
        base = g * PLANE
        live = []
        for i in range(PLANE):
            live.append(jnp.where(slot < count[0, 0, base + i], weight[base + i], 0.0))
            weight[base + i] = live[i]
        w = stack(live)
        high, low = star_codes(stack([star[base + i] for i in range(PLANE)]))
        value = w * stack([magnitude[base + i] for i in range(PLANE)])
        return total + scatter(high, low, two_parts(w) + two_parts(value), 128, 32)

    total = lax.fori_loop(0, n_exp // PLANE, first, jnp.zeros((128, 128), f32))
    wsum[...] = prior + star_table(total[:, :64])
    mean[...] = star_table(total[:, 64:]) / wsum[...]

    pl.semaphore_wait(barrier, n_exp - 1 + n_sky - 1)

    def exchange(phase, block, turned):
        @pl.loop(0, CHIPS // 2)
        def _(pair):
            todo = []
            for u in range(2):
                q = CHIPS - 1 - 2 * pair - u if turned else 2 * pair + u
                base = member(q, 1)
                for core in (partner, my_c):
                    j = base + core
                    todo.append((j, q, core is my_c and u == (1 if turned else 0)))
            made = [block(j) for j, _, _ in todo]
            for (j, _, _), x in zip(todo, made):
                sent[phase, j] = x
            for j, q, maybe_own in todo:
                def send(j=j, q=q):
                    pltpu.make_async_remote_copy(
                        src_ref=sent.at[phase, j], dst_ref=got.at[phase, me],
                        send_sem=sends.at[phase], recv_sem=arrivals.at[phase, q // 4],
                        device_id={"exp": j}, device_id_type=MESH).start()

                if maybe_own:
                    pl.when(q != 0)(send)

                    @pl.when(q == 0)
                    def _():
                        pltpu.make_async_copy(sent.at[phase, me], got.at[phase, me], arrivals.at[phase, 0]).start()
                else:
                    send()

    def arrive(phase, group):
        pltpu.make_async_copy(
            sent.at[phase, pl.ds(0, PLANE)], got.at[phase, pl.ds(0, PLANE)], arrivals.at[phase, group]).wait()

    def over_groups(phase, shape, turned, part):
        def one(step, total):
            group = CHIPS // 4 - 1 - step if turned else step
            js = []
            for u in range(4):
                base = member(4 * group + u, -1)
                js += [base, base + 1]
            arrive(phase, group)
            return total + part(js)

        return lax.fori_loop(0, CHIPS // 4, one, jnp.zeros(shape, f32))

    def to_owners(phase, values):
        exchange(phase, lambda j: weight[j] * (values(j) - pick(mean, STAR_ROWS, star[j])), False)

    def star_means(phase):
        def part(js):
            high, low = star_codes(stack([star[j] for j in js]))
            value = stack([weight[j] for j in js]) * stack([got[phase, j] for j in js])
            return scatter(high, low, two_parts(value), 128, 32)

        mean[...] = star_table(over_groups(phase, (128, 64), True, part)) / wsum[...]

    def owner_sums(phase, turn, before_sending=lambda: None):
        def part(js):
            high, low = zp_codes(stack([zp[j] for j in js]))
            return scatter(high, low, two_parts(stack([got[phase, j] for j in js])), 2 * ZP_PAD, 64)

        total = over_groups(phase, (2 * ZP_PAD, LANES), False, part)
        both = total + pltpu.roll(total, 64, 1)
        lane = lax.broadcasted_iota(jnp.int32, (ZP_PAD, LANES), 1)
        shares[turn, sky, pl.ds(0, ZP_PAD)] = jnp.where(lane < 64, both[:ZP_PAD], both[ZP_PAD:])
        before_sending()
        for t in (2, 1, 3):
            pltpu.make_async_remote_copy(
                src_ref=shares.at[turn, sky], dst_ref=shares.at[turn, sky],
                send_sem=sends.at[5 + turn], recv_sem=arrivals.at[5 + turn, 0],
                device_id={"sky": lax.rem(sky + t, n_sky)}, device_id_type=MESH).start()
        pltpu.make_async_copy(
            shares.at[turn, pl.ds(0, 3)], shares.at[turn, pl.ds(0, 3)], arrivals.at[5 + turn, 0]).wait()
        part = [shares[turn, i, pl.ds(0, ZP_PAD)] for i in range(4)]
        return (part[0] + part[1]) + (part[2] + part[3])

    def put_dots(turn, rows):
        dots[turn, me] = stack(rows + [jnp.zeros((1, LANES), f32)] * (SUB - len(rows)))

        @pl.loop(1, n_exp)
        def _(t):
            pltpu.make_async_remote_copy(
                src_ref=dots.at[turn, me], dst_ref=dots.at[turn, me],
                send_sem=sends.at[8 + turn], recv_sem=arrivals.at[8 + turn, 0],
                device_id={"exp": lax.rem(me + t, n_exp)}, device_id_type=MESH).start()

    def take_dots(turn):
        pltpu.make_async_copy(
            dots.at[turn, pl.ds(0, n_exp - 1)], dots.at[turn, pl.ds(0, n_exp - 1)], arrivals.at[8 + turn, 0]).wait()
        return jnp.sum(dots[turn], axis=0)

    def column(x):
        return jnp.sum(x, axis=0, keepdims=True)

    to_owners(0, lambda j: magnitude[j])
    for copy in incoming[3 * SUB :]:
        copy.wait()
    for turn in range(3):
        shares[turn, sky, pl.ds(ZP_PAD, SUB)] = jnp.zeros((SUB, LANES), f32)
    fields[0] = owner_sums(0, 0)

    @pl.loop(0, 2)
    def _(turn):
        taken, given = 2 * turn + 1, 2 * turn + 2
        exchange(taken, lambda k: pick(fields.at[turn], ZP_ROWS, zp[k]), True)

        @pl.when(turn == 1)
        def _():
            b, c = fields[0], fields[1]
            put_dots(0, [column(b * b), column(b * c)])

        star_means(taken)
        to_owners(given, lambda j: got[taken, j])

        @pl.when(turn == 1)
        def _():
            sums = jnp.sum(take_dots(0), axis=1, keepdims=True)
            alpha = jnp.broadcast_to(sums[0:1] / sums[1:2], (1, LANES))
            scale[0:1] = alpha
            scale[1:2] = jnp.broadcast_to(sums[0:1], (1, LANES))
            b, c = fields[0], fields[1]
            r = b - alpha * c
            slots = [jnp.zeros((SUB, LANES), f32)] * 3

            def add(j, slots):
                v, t = got[1, j], sent[2, j]
                w, s = v - alpha * got[3, j], t - alpha * sent[4, j]
                return [slots[0] + w * s, slots[1] + v * s, slots[2] + v * t]

            slots = lax.fori_loop(0, n_exp, add, slots, unroll=4)
            put_dots(1, [column(x) for x in slots] + [column(r * r), column(r * b)])

        def with_dots():
            @pl.when(turn == 1)
            def _():
                shares[2, sky, pl.ds(ZP_PAD, SUB)] = take_dots(1)

        fields[turn + 1] = owner_sums(given, turn + 1, with_dots) + ridge * fields[turn]

    b, c, d = fields[0], fields[1], fields[2]
    alpha, norm_now = scale[0:1], scale[1:2]
    last = [shares[2, i, pl.ds(ZP_PAD, SUB)] for i in range(4)]
    sums = jnp.broadcast_to(jnp.sum((last[0] + last[1]) + (last[2] + last[3]), axis=1, keepdims=True), (SUB, LANES))
    norm_next, cross = 0.25 * sums[3:4], 0.25 * sums[4:5]
    ratio = norm_next / norm_now
    square = norm_next + 2.0 * ratio * cross + ratio * ratio * norm_now
    curve = ridge * square + (sums[0:1] + 2.0 * ratio * sums[1:2] + ratio * ratio * sums[2:3])
    step = norm_next / curve
    r = b - alpha * c
    x_out[...] = alpha * b + step * (r + ratio * b)
    r_out[...] = r - step * ((c - alpha * d) + ratio * c)

    for phase in range(5):
        pltpu.make_async_copy(
            sent.at[phase, pl.ds(0, n_exp - 1)], got.at[phase, pl.ds(0, n_exp - 1)], sends.at[phase]).wait()
    for turn in range(3):
        pltpu.make_async_copy(
            shares.at[turn, pl.ds(0, 3)], shares.at[turn, pl.ds(0, 3)], sends.at[5 + turn]).wait()
    for turn in range(2):
        pltpu.make_async_copy(
            dots.at[turn, pl.ds(0, n_exp - 1)], dots.at[turn, pl.ds(0, n_exp - 1)], sends.at[8 + turn]).wait()


def body(obs_weight, magnitude, star_id, peer_count, zp_index):
    n_sky, n_exp = lax.axis_size("sky"), lax.axis_size("exp")
    blocks = (n_exp, SUB, LANES)
    owned = jax.ShapeDtypeStruct((ZP_PAD, LANES), f32)
    anywhere = pl.BlockSpec(memory_space=pl.ANY)
    inside = pl.BlockSpec(memory_space=pltpu.VMEM)
    x, r = pl.pallas_call(
        functools.partial(kernel, n_sky, n_exp),
        out_shape=(owned, owned),
        in_specs=[pl.BlockSpec(memory_space=pltpu.SMEM)] + [anywhere] * 4,
        out_specs=(inside, inside),
        scratch_shapes=[
            pltpu.VMEM(blocks, f32),
            pltpu.VMEM(blocks, f32),
            pltpu.VMEM(blocks, jnp.int32),
            pltpu.VMEM(blocks, jnp.int32),
            pltpu.VMEM((STAR_ROWS, LANES), f32),
            pltpu.VMEM((STAR_ROWS, LANES), f32),
            pltpu.VMEM((3, ZP_PAD, LANES), f32),
            pltpu.VMEM((SUB, LANES), f32),
            pltpu.VMEM((5,) + blocks, f32),
            pltpu.VMEM((5,) + blocks, f32),
            pltpu.VMEM((3, n_sky, ZP_PAD + SUB, LANES), f32),
            pltpu.VMEM((2, n_exp, SUB, LANES), f32),
            pltpu.SemaphoreType.DMA((4, SUB)),
            pltpu.SemaphoreType.DMA((10,)),
            pltpu.SemaphoreType.DMA((10, CHIPS // 4)),
        ],
        compiler_params=pltpu.CompilerParams(collective_id=0, has_side_effects=True),
        name="ubercal_cg",
    )(peer_count, obs_weight, magnitude, star_id, zp_index)
    return x.reshape(-1)[:ZP_DEV], r.reshape(-1)[:ZP_DEV]


def solution(mesh):
    return jax.shard_map(
        body,
        mesh=mesh,
        in_specs=(
            P("sky", "exp", None, None),
            P("sky", "exp", None, None),
            P("sky", "exp", None, None),
            P("sky", "exp", None),
            P("sky", "exp", None, None),
        ),
        out_specs=(P("exp"), P("exp")),
        check_vma=False,
    )
```

```python
import functools

import jax
import jax.numpy as jnp
from jax import lax
from jax.experimental import pallas as pl
from jax.experimental.pallas import tpu as pltpu
from jax.sharding import PartitionSpec as P

CAP = 1024
STAR_DEV = 4096
ZP_DEV = 12096
LANES = 128
SUB = CAP // LANES
STAR_ROWS = STAR_DEV // LANES
ZP_ROWS = (ZP_DEV + LANES - 1) // LANES
ZP_PAD = 96
PLANE = 8

OFFSETS = ((0, 0), (0, 1), (0, 3), (1, 0), (3, 0), (1, 1), (0, 2), (2, 0),
           (1, 3), (3, 1), (3, 3), (2, 1), (2, 2), (2, 3), (1, 2), (3, 2))
CHIPS = len(OFFSETS)


def digits(values):
    code = sum(v << (2 * q) for q, v in enumerate(values))
    return code - (1 << 32) if code >= 1 << 31 else code


OFFSET_Z = digits([z for z, _ in OFFSETS])
OFFSET_Y = digits([y for _, y in OFFSETS])

ridge = 1.0
prior = 1.0
f32 = jnp.float32
bf16 = jnp.bfloat16
NT = (((1,), (1,)), ((), ()))
MESH = pl.DeviceIdType.MESH


def two_parts(x):
    coarse = x.astype(bf16)
    return coarse, (x - coarse.astype(f32)).astype(bf16)


def as_code(x):
    return x.astype(f32).astype(bf16)


def row_of(x, r, n):
    return jnp.broadcast_to(x[r : r + 1, :], (n, LANES))


def scatter(high, low, parts, n_high, n_low):
    rows = high.shape[0]
    iota_high = as_code(lax.broadcasted_iota(jnp.int32, (n_high, LANES), 0))
    iota_low = as_code(lax.broadcasted_iota(jnp.int32, (n_low, LANES), 0))
    one, zero = jnp.ones((), bf16), jnp.zeros((), bf16)
    hot, weighted = [], [[] for _ in parts]
    for r in range(rows):
        hot.append(jnp.where(row_of(high, r, n_high) == iota_high, one, zero))
        mask = row_of(low, r, n_low) == iota_low
        for column, part in zip(weighted, parts):
            column.append(jnp.where(mask, row_of(part, r, n_low), zero))
    hot = jnp.concatenate(hot, axis=1)
    weighted = jnp.concatenate([jnp.concatenate(c, axis=1) for c in weighted], axis=0)
    return lax.dot_general(hot, weighted, NT, preferred_element_type=f32)


def pick(table, rows, index):
    high, low = lax.shift_right_logical(index, 7), index & 127
    found = jnp.zeros(index.shape, f32)
    for r in range(rows):
        line = jnp.broadcast_to(table[r : r + 1, :], index.shape)
        found = jnp.where(high == r, jnp.take_along_axis(line, low, axis=1), found)
    return found


def star_codes(index):
    high = lax.shift_right_logical(index, 7) + STAR_ROWS * (lax.shift_right_logical(index, 5) & 3)
    return as_code(high), as_code(index & 31)


def zp_codes(index):
    high = lax.shift_right_logical(index, 7) + ZP_PAD * (lax.shift_right_logical(index, 6) & 1)
    return as_code(high), as_code(index & 63)


def star_table(pair):
    both = pair[:, :32] + pair[:, 32:64]
    return jnp.concatenate([both[32 * q : 32 * q + 32, :] for q in range(4)], axis=1)


def kernel(
    n_sky, n_exp,
    count, weight_in, magnitude_in, star_in, zp_in,
    x_out, r_out,
    weight, magnitude, star, zp, wsum, mean, fields, scale,
    sent, got, shares, dots, loads, sends, arrivals,
):
    sky, me = lax.axis_index("sky"), lax.axis_index("exp")
    my_z, my_y, my_c = me // 8, (me // 2) % 4, me % 2
    partner = 1 - my_c

    def digit(code, q):
        return lax.shift_right_logical(jnp.int32(code), 2 * q) & 3

    def member(q, sign):
        z = (my_z + 4 + sign * digit(OFFSET_Z, q)) & 3
        y = (my_y + 4 + sign * digit(OFFSET_Y, q)) & 3
        return z * 8 + y * 2

    incoming = []
    for a, (source, target) in enumerate(((weight_in, weight), (star_in, star), (magnitude_in, magnitude), (zp_in, zp))):
        for c in range(SUB):
            copy = pltpu.make_async_copy(
                source.at[0, 0, :, pl.ds(c * LANES, LANES)], target.at[:, c, :], loads.at[a, c])
            copy.start()
            incoming.append(copy)

    barrier = pltpu.get_barrier_semaphore()

    @pl.loop(1, n_exp)
    def _(t):
        pl.semaphore_signal(barrier, inc=1, device_id={"exp": lax.rem(me + t, n_exp)}, device_id_type=MESH)

    for t in range(1, n_sky):
        pl.semaphore_signal(barrier, inc=1, device_id={"sky": lax.rem(sky + t, n_sky)}, device_id_type=MESH)

    for copy in incoming[: 3 * SUB]:
        copy.wait()

    slot = lax.broadcasted_iota(jnp.int32, (SUB, LANES), 0) * LANES + lax.broadcasted_iota(jnp.int32, (SUB, LANES), 1)

    def stack(blocks):
        return jnp.concatenate(blocks, axis=0)

    def first(g, total):
        base = g * PLANE
        live = []
        for i in range(PLANE):
            live.append(jnp.where(slot < count[0, 0, base + i], weight[base + i], 0.0))
            weight[base + i] = live[i]
        w = stack(live)
        high, low = star_codes(stack([star[base + i] for i in range(PLANE)]))
        value = w * stack([magnitude[base + i] for i in range(PLANE)])
        return total + scatter(high, low, two_parts(w) + two_parts(value), 128, 32)

    total = lax.fori_loop(0, n_exp // PLANE, first, jnp.zeros((128, 128), f32))
    wsum[...] = prior + star_table(total[:, :64])
    mean[...] = star_table(total[:, 64:]) / wsum[...]

    pl.semaphore_wait(barrier, n_exp - 1 + n_sky - 1)

    def exchange(phase, block, turned):
        @pl.loop(0, CHIPS // 2)
        def _(pair):
            todo = []
            for u in range(2):
                q = CHIPS - 1 - 2 * pair - u if turned else 2 * pair + u
                base = member(q, 1)
                for core in (partner, my_c):
                    j = base + core
                    todo.append((j, q, core is my_c and u == (1 if turned else 0)))
            made = [block(j) for j, _, _ in todo]
            for (j, _, _), x in zip(todo, made):
                sent[phase, j] = x
            for j, q, maybe_own in todo:
                def send(j=j, q=q):
                    pltpu.make_async_remote_copy(
                        src_ref=sent.at[phase, j], dst_ref=got.at[phase, me],
                        send_sem=sends.at[phase], recv_sem=arrivals.at[phase, q // 4],
                        device_id={"exp": j}, device_id_type=MESH).start()

                if maybe_own:
                    pl.when(q != 0)(send)

                    @pl.when(q == 0)
                    def _():
                        pltpu.make_async_copy(sent.at[phase, me], got.at[phase, me], arrivals.at[phase, 0]).start()
                else:
                    send()

    def arrive(phase, group):
        pltpu.make_async_copy(
            sent.at[phase, pl.ds(0, PLANE)], got.at[phase, pl.ds(0, PLANE)], arrivals.at[phase, group]).wait()

    def over_groups(phase, shape, turned, part):
        def one(step, total):
            group = CHIPS // 4 - 1 - step if turned else step
            js = []
            for u in range(4):
                base = member(4 * group + u, -1)
                js += [base, base + 1]
            arrive(phase, group)
            return total + part(js)

        return lax.fori_loop(0, CHIPS // 4, one, jnp.zeros(shape, f32))

    def to_owners(phase, values):
        exchange(phase, lambda j: weight[j] * (values(j) - pick(mean, STAR_ROWS, star[j])), False)

    def star_means(phase):
        def part(js):
            high, low = star_codes(stack([star[j] for j in js]))
            value = stack([weight[j] for j in js]) * stack([got[phase, j] for j in js])
            return scatter(high, low, two_parts(value), 128, 32)

        mean[...] = star_table(over_groups(phase, (128, 64), True, part)) / wsum[...]

    def owner_sums(phase, turn, before_sending=lambda: None):
        def part(js):
            high, low = zp_codes(stack([zp[j] for j in js]))
            return scatter(high, low, two_parts(stack([got[phase, j] for j in js])), 2 * ZP_PAD, 64)

        total = over_groups(phase, (2 * ZP_PAD, LANES), False, part)
        both = total + pltpu.roll(total, 64, 1)
        lane = lax.broadcasted_iota(jnp.int32, (ZP_PAD, LANES), 1)
        shares[turn, sky, pl.ds(0, ZP_PAD)] = jnp.where(lane < 64, both[:ZP_PAD], both[ZP_PAD:])
        before_sending()
        for t in (2, 1, 3):
            pltpu.make_async_remote_copy(
                src_ref=shares.at[turn, sky], dst_ref=shares.at[turn, sky],
                send_sem=sends.at[5 + turn], recv_sem=arrivals.at[5 + turn, 0],
                device_id={"sky": lax.rem(sky + t, n_sky)}, device_id_type=MESH).start()
        pltpu.make_async_copy(
            shares.at[turn, pl.ds(0, 3)], shares.at[turn, pl.ds(0, 3)], arrivals.at[5 + turn, 0]).wait()
        part = [shares[turn, i, pl.ds(0, ZP_PAD)] for i in range(4)]
        return (part[0] + part[1]) + (part[2] + part[3])

    def put_dots(turn, rows):
        dots[turn, me] = stack(rows + [jnp.zeros((1, LANES), f32)] * (SUB - len(rows)))

        @pl.loop(1, n_exp)
        def _(t):
            pltpu.make_async_remote_copy(
                src_ref=dots.at[turn, me], dst_ref=dots.at[turn, me],
                send_sem=sends.at[8 + turn], recv_sem=arrivals.at[8 + turn, 0],
                device_id={"exp": lax.rem(me + t, n_exp)}, device_id_type=MESH).start()

    def take_dots(turn):
        pltpu.make_async_copy(
            dots.at[turn, pl.ds(0, n_exp - 1)], dots.at[turn, pl.ds(0, n_exp - 1)], arrivals.at[8 + turn, 0]).wait()
        return jnp.sum(dots[turn], axis=0)

    def column(x):
        return jnp.sum(x, axis=0, keepdims=True)

    to_owners(0, lambda j: magnitude[j])
    for copy in incoming[3 * SUB :]:
        copy.wait()
    for turn in range(3):
        shares[turn, sky, pl.ds(ZP_PAD, SUB)] = jnp.zeros((SUB, LANES), f32)
    fields[0] = owner_sums(0, 0)

    @pl.loop(0, 2)
    def _(turn):
        taken, given = 2 * turn + 1, 2 * turn + 2
        exchange(taken, lambda k: pick(fields.at[turn], ZP_ROWS, zp[k]), True)

        @pl.when(turn == 1)
        def _():
            b, c = fields[0], fields[1]
            put_dots(0, [column(b * b), column(b * c)])

        star_means(taken)
        to_owners(given, lambda j: got[taken, j])

        @pl.when(turn == 1)
        def _():
            sums = jnp.sum(take_dots(0), axis=1, keepdims=True)
            alpha = jnp.broadcast_to(sums[0:1] / sums[1:2], (1, LANES))
            scale[0:1] = alpha
            scale[1:2] = jnp.broadcast_to(sums[0:1], (1, LANES))
            b, c = fields[0], fields[1]
            r = b - alpha * c
            slots = [jnp.zeros((SUB, LANES), f32)] * 3

            def add(j, slots):
                v, t = got[1, j], sent[2, j]
                w, s = v - alpha * got[3, j], t - alpha * sent[4, j]
                return [slots[0] + w * s, slots[1] + v * s, slots[2] + v * t]

            slots = lax.fori_loop(0, n_exp, add, slots, unroll=4)
            put_dots(1, [column(x) for x in slots] + [column(r * r), column(r * b)])

        def with_dots():
            @pl.when(turn == 1)
            def _():
                shares[2, sky, pl.ds(ZP_PAD, SUB)] = take_dots(1)

        fields[turn + 1] = owner_sums(given, turn + 1, with_dots) + ridge * fields[turn]

    b, c, d = fields[0], fields[1], fields[2]
    alpha, norm_now = scale[0:1], scale[1:2]
    last = [shares[2, i, pl.ds(ZP_PAD, SUB)] for i in range(4)]
    sums = jnp.broadcast_to(jnp.sum((last[0] + last[1]) + (last[2] + last[3]), axis=1, keepdims=True), (SUB, LANES))
    norm_next, cross = 0.25 * sums[3:4], 0.25 * sums[4:5]
    ratio = norm_next / norm_now
    square = norm_next + 2.0 * ratio * cross + ratio * ratio * norm_now
    curve = ridge * square + (sums[0:1] + 2.0 * ratio * sums[1:2] + ratio * ratio * sums[2:3])
    step = norm_next / curve
    r = b - alpha * c
    x_out[...] = alpha * b + step * (r + ratio * b)
    r_out[...] = r - step * ((c - alpha * d) + ratio * c)

    for phase in range(5):
        pltpu.make_async_copy(
            sent.at[phase, pl.ds(0, n_exp - 1)], got.at[phase, pl.ds(0, n_exp - 1)], sends.at[phase]).wait()
    for turn in range(3):
        pltpu.make_async_copy(
            shares.at[turn, pl.ds(0, 3)], shares.at[turn, pl.ds(0, 3)], sends.at[5 + turn]).wait()
    for turn in range(2):
        pltpu.make_async_copy(
            dots.at[turn, pl.ds(0, n_exp - 1)], dots.at[turn, pl.ds(0, n_exp - 1)], sends.at[8 + turn]).wait()


def body(obs_weight, magnitude, star_id, peer_count, zp_index):
    n_sky, n_exp = lax.axis_size("sky"), lax.axis_size("exp")
    blocks = (n_exp, SUB, LANES)
    owned = pltpu.VMEM((ZP_PAD, LANES), f32)
    anywhere = pl.BlockSpec(memory_space=pl.ANY)
    inside = pl.BlockSpec(memory_space=pltpu.VMEM)
    x, r = pl.pallas_call(
        functools.partial(kernel, n_sky, n_exp),
        out_shape=(owned, owned),
        in_specs=[pl.BlockSpec(memory_space=pltpu.SMEM)] + [anywhere] * 4,
        out_specs=(inside, inside),
        scratch_shapes=[
            pltpu.VMEM(blocks, f32),
            pltpu.VMEM(blocks, f32),
            pltpu.VMEM(blocks, jnp.int32),
            pltpu.VMEM(blocks, jnp.int32),
            pltpu.VMEM((STAR_ROWS, LANES), f32),
            pltpu.VMEM((STAR_ROWS, LANES), f32),
            pltpu.VMEM((3, ZP_PAD, LANES), f32),
            pltpu.VMEM((SUB, LANES), f32),
            pltpu.VMEM((5,) + blocks, f32),
            pltpu.VMEM((5,) + blocks, f32),
            pltpu.VMEM((3, n_sky, ZP_PAD + SUB, LANES), f32),
            pltpu.VMEM((2, n_exp, SUB, LANES), f32),
            pltpu.SemaphoreType.DMA((4, SUB)),
            pltpu.SemaphoreType.DMA((10,)),
            pltpu.SemaphoreType.DMA((10, CHIPS // 4)),
        ],
        compiler_params=pltpu.CompilerParams(collective_id=0, has_side_effects=True),
        name="ubercal_cg",
    )(peer_count, obs_weight, magnitude, star_id, zp_index)
    return x.reshape(-1)[:ZP_DEV], r.reshape(-1)[:ZP_DEV]


def solution(mesh):
    return jax.shard_map(
        body,
        mesh=mesh,
        in_specs=(
            P("sky", "exp", None, None),
            P("sky", "exp", None, None),
            P("sky", "exp", None, None),
            P("sky", "exp", None),
            P("sky", "exp", None, None),
        ),
        out_specs=(P("exp"), P("exp")),
        check_vma=False,
    )
```

```python
import functools

import jax
import jax.numpy as jnp
from jax import lax
from jax.experimental import pallas as pl
from jax.experimental.pallas import tpu as pltpu
from jax.sharding import PartitionSpec as P

CAP = 1024
STAR_DEV = 4096
ZP_DEV = 12096
LANES = 128
SUB = CAP // LANES
STAR_ROWS = STAR_DEV // LANES
ZP_ROWS = (ZP_DEV + LANES - 1) // LANES
ZP_PAD = 96
PLANE = 8

OFFSETS = ((0, 0), (0, 1), (0, 3), (1, 0), (3, 0), (1, 1), (0, 2), (2, 0),
           (1, 3), (3, 1), (3, 3), (2, 1), (2, 2), (2, 3), (1, 2), (3, 2))
CHIPS = len(OFFSETS)


def digits(values):
    code = sum(v << (2 * q) for q, v in enumerate(values))
    return code - (1 << 32) if code >= 1 << 31 else code


OFFSET_Z = digits([z for z, _ in OFFSETS])
OFFSET_Y = digits([y for _, y in OFFSETS])

ridge = 1.0
prior = 1.0
f32 = jnp.float32
bf16 = jnp.bfloat16
NT = (((1,), (1,)), ((), ()))
MESH = pl.DeviceIdType.MESH


def two_parts(x):
    coarse = x.astype(bf16)
    return coarse, (x - coarse.astype(f32)).astype(bf16)


def as_code(x):
    return x.astype(f32).astype(bf16)


def row_of(x, r, n):
    return jnp.broadcast_to(x[r : r + 1, :], (n, LANES))


def scatter(high, low, parts, n_high, n_low):
    rows = high.shape[0]
    iota_high = as_code(lax.broadcasted_iota(jnp.int32, (n_high, LANES), 0))
    iota_low = as_code(lax.broadcasted_iota(jnp.int32, (n_low, LANES), 0))
    one, zero = jnp.ones((), bf16), jnp.zeros((), bf16)
    hot, weighted = [], [[] for _ in parts]
    for r in range(rows):
        hot.append(jnp.where(row_of(high, r, n_high) == iota_high, one, zero))
        mask = row_of(low, r, n_low) == iota_low
        for column, part in zip(weighted, parts):
            column.append(jnp.where(mask, row_of(part, r, n_low), zero))
    hot = jnp.concatenate(hot, axis=1)
    weighted = jnp.concatenate([jnp.concatenate(c, axis=1) for c in weighted], axis=0)
    return lax.dot_general(hot, weighted, NT, preferred_element_type=f32)


def pick(table, rows, index):
    high, low = lax.shift_right_logical(index, 7), index & 127
    found = jnp.zeros(index.shape, f32)
    for r in range(rows):
        line = jnp.broadcast_to(table[r : r + 1, :], index.shape)
        found = jnp.where(high == r, jnp.take_along_axis(line, low, axis=1), found)
    return found


def star_codes(index):
    high = lax.shift_right_logical(index, 7) + STAR_ROWS * (lax.shift_right_logical(index, 5) & 3)
    return as_code(high), as_code(index & 31)


def zp_codes(index):
    high = lax.shift_right_logical(index, 7) + ZP_PAD * (lax.shift_right_logical(index, 6) & 1)
    return as_code(high), as_code(index & 63)


def star_table(pair):
    both = pair[:, :32] + pair[:, 32:64]
    return jnp.concatenate([both[32 * q : 32 * q + 32, :] for q in range(4)], axis=1)


def kernel(
    n_sky, n_exp,
    count, weight_in, magnitude_in, star_in, zp_in,
    out,
    weight, magnitude, star, zp, wsum, mean, fields, scale,
    sent, got, shares, dots, loads, sends, arrivals,
):
    sky, me = lax.axis_index("sky"), lax.axis_index("exp")
    my_z, my_y, my_c = me // 8, (me // 2) % 4, me % 2
    partner = 1 - my_c

    def digit(code, q):
        return lax.shift_right_logical(jnp.int32(code), 2 * q) & 3

    def member(q, sign):
        z = (my_z + 4 + sign * digit(OFFSET_Z, q)) & 3
        y = (my_y + 4 + sign * digit(OFFSET_Y, q)) & 3
        return z * 8 + y * 2

    incoming = []
    for a, (source, target) in enumerate(((weight_in, weight), (star_in, star), (magnitude_in, magnitude), (zp_in, zp))):
        for c in range(SUB):
            copy = pltpu.make_async_copy(
                source.at[0, 0, :, pl.ds(c * LANES, LANES)], target.at[:, c, :], loads.at[a, c])
            copy.start()
            incoming.append(copy)

    barrier = pltpu.get_barrier_semaphore()

    @pl.loop(1, n_exp)
    def _(t):
        pl.semaphore_signal(barrier, inc=1, device_id={"exp": lax.rem(me + t, n_exp)}, device_id_type=MESH)

    for t in range(1, n_sky):
        pl.semaphore_signal(barrier, inc=1, device_id={"sky": lax.rem(sky + t, n_sky)}, device_id_type=MESH)

    for copy in incoming[: 3 * SUB]:
        copy.wait()

    slot = lax.broadcasted_iota(jnp.int32, (SUB, LANES), 0) * LANES + lax.broadcasted_iota(jnp.int32, (SUB, LANES), 1)

    def stack(blocks):
        return jnp.concatenate(blocks, axis=0)

    def first(g, total):
        base = g * PLANE
        live = []
        for i in range(PLANE):
            live.append(jnp.where(slot < count[0, 0, base + i], weight[base + i], 0.0))
            weight[base + i] = live[i]
        w = stack(live)
        high, low = star_codes(stack([star[base + i] for i in range(PLANE)]))
        value = w * stack([magnitude[base + i] for i in range(PLANE)])
        return total + scatter(high, low, two_parts(w) + two_parts(value), 128, 32)

    total = lax.fori_loop(0, n_exp // PLANE, first, jnp.zeros((128, 128), f32))
    wsum[...] = prior + star_table(total[:, :64])
    mean[...] = star_table(total[:, 64:]) / wsum[...]

    pl.semaphore_wait(barrier, n_exp - 1 + n_sky - 1)

    def exchange(phase, block, turned):
        @pl.loop(0, CHIPS // 2)
        def _(pair):
            todo = []
            for u in range(2):
                q = CHIPS - 1 - 2 * pair - u if turned else 2 * pair + u
                base = member(q, 1)
                for core in (partner, my_c):
                    j = base + core
                    todo.append((j, q, core is my_c and u == (1 if turned else 0)))
            made = [block(j) for j, _, _ in todo]
            for (j, _, _), x in zip(todo, made):
                sent[phase, j] = x
            for j, q, maybe_own in todo:
                def send(j=j, q=q):
                    pltpu.make_async_remote_copy(
                        src_ref=sent.at[phase, j], dst_ref=got.at[phase, me],
                        send_sem=sends.at[phase], recv_sem=arrivals.at[phase, q // 4],
                        device_id={"exp": j}, device_id_type=MESH).start()

                if maybe_own:
                    pl.when(q != 0)(send)

                    @pl.when(q == 0)
                    def _():
                        pltpu.make_async_copy(sent.at[phase, me], got.at[phase, me], arrivals.at[phase, 0]).start()
                else:
                    send()

    def arrive(phase, group):
        pltpu.make_async_copy(
            sent.at[phase, pl.ds(0, PLANE)], got.at[phase, pl.ds(0, PLANE)], arrivals.at[phase, group]).wait()

    def over_groups(phase, shape, turned, part):
        def one(step, total):
            group = CHIPS // 4 - 1 - step if turned else step
            js = []
            for u in range(4):
                base = member(4 * group + u, -1)
                js += [base, base + 1]
            arrive(phase, group)
            return total + part(js)

        return lax.fori_loop(0, CHIPS // 4, one, jnp.zeros(shape, f32))

    def to_owners(phase, values):
        exchange(phase, lambda j: weight[j] * (values(j) - pick(mean, STAR_ROWS, star[j])), False)

    def star_means(phase):
        def part(js):
            high, low = star_codes(stack([star[j] for j in js]))
            value = stack([weight[j] for j in js]) * stack([got[phase, j] for j in js])
            return scatter(high, low, two_parts(value), 128, 32)

        mean[...] = star_table(over_groups(phase, (128, 64), True, part)) / wsum[...]

    def owner_sums(phase, turn, before_sending=lambda: None):
        def part(js):
            high, low = zp_codes(stack([zp[j] for j in js]))
            return scatter(high, low, two_parts(stack([got[phase, j] for j in js])), 2 * ZP_PAD, 64)

        total = over_groups(phase, (2 * ZP_PAD, LANES), False, part)
        both = total + pltpu.roll(total, 64, 1)
        lane = lax.broadcasted_iota(jnp.int32, (ZP_PAD, LANES), 1)
        shares[turn, sky, pl.ds(0, ZP_PAD)] = jnp.where(lane < 64, both[:ZP_PAD], both[ZP_PAD:])
        before_sending()
        for t in (2, 1, 3):
            pltpu.make_async_remote_copy(
                src_ref=shares.at[turn, sky], dst_ref=shares.at[turn, sky],
                send_sem=sends.at[5 + turn], recv_sem=arrivals.at[5 + turn, 0],
                device_id={"sky": lax.rem(sky + t, n_sky)}, device_id_type=MESH).start()
        pltpu.make_async_copy(
            shares.at[turn, pl.ds(0, 3)], shares.at[turn, pl.ds(0, 3)], arrivals.at[5 + turn, 0]).wait()
        part = [shares[turn, i, pl.ds(0, ZP_PAD)] for i in range(4)]
        return (part[0] + part[1]) + (part[2] + part[3])

    def put_dots(turn, rows):
        dots[turn, me] = stack(rows + [jnp.zeros((1, LANES), f32)] * (SUB - len(rows)))

        @pl.loop(1, n_exp)
        def _(t):
            pltpu.make_async_remote_copy(
                src_ref=dots.at[turn, me], dst_ref=dots.at[turn, me],
                send_sem=sends.at[8 + turn], recv_sem=arrivals.at[8 + turn, 0],
                device_id={"exp": lax.rem(me + t, n_exp)}, device_id_type=MESH).start()

    def take_dots(turn):
        pltpu.make_async_copy(
            dots.at[turn, pl.ds(0, n_exp - 1)], dots.at[turn, pl.ds(0, n_exp - 1)], arrivals.at[8 + turn, 0]).wait()
        return jnp.sum(dots[turn], axis=0)

    def column(x):
        return jnp.sum(x, axis=0, keepdims=True)

    to_owners(0, lambda j: magnitude[j])
    for copy in incoming[3 * SUB :]:
        copy.wait()
    for turn in range(3):
        shares[turn, sky, pl.ds(ZP_PAD, SUB)] = jnp.zeros((SUB, LANES), f32)
    fields[0] = owner_sums(0, 0)

    @pl.loop(0, 2)
    def _(turn):
        taken, given = 2 * turn + 1, 2 * turn + 2
        exchange(taken, lambda k: pick(fields.at[turn], ZP_ROWS, zp[k]), True)

        @pl.when(turn == 1)
        def _():
            b, c = fields[0], fields[1]
            put_dots(0, [column(b * b), column(b * c)])

        star_means(taken)
        to_owners(given, lambda j: got[taken, j])

        @pl.when(turn == 1)
        def _():
            sums = jnp.sum(take_dots(0), axis=1, keepdims=True)
            alpha = jnp.broadcast_to(sums[0:1] / sums[1:2], (1, LANES))
            scale[0:1] = alpha
            scale[1:2] = jnp.broadcast_to(sums[0:1], (1, LANES))
            b, c = fields[0], fields[1]
            r = b - alpha * c
            slots = [jnp.zeros((SUB, LANES), f32)] * 3

            def add(j, slots):
                v, t = got[1, j], sent[2, j]
                w, s = v - alpha * got[3, j], t - alpha * sent[4, j]
                return [slots[0] + w * s, slots[1] + v * s, slots[2] + v * t]

            slots = lax.fori_loop(0, n_exp, add, slots, unroll=4)
            put_dots(1, [column(x) for x in slots] + [column(r * r), column(r * b)])

        def with_dots():
            @pl.when(turn == 1)
            def _():
                shares[2, sky, pl.ds(ZP_PAD, SUB)] = take_dots(1)

        fields[turn + 1] = owner_sums(given, turn + 1, with_dots) + ridge * fields[turn]

    b, c, d = fields[0], fields[1], fields[2]
    alpha, norm_now = scale[0:1], scale[1:2]
    last = [shares[2, i, pl.ds(ZP_PAD, SUB)] for i in range(4)]
    sums = jnp.broadcast_to(jnp.sum((last[0] + last[1]) + (last[2] + last[3]), axis=1, keepdims=True), (SUB, LANES))
    norm_next, cross = 0.25 * sums[3:4], 0.25 * sums[4:5]
    ratio = norm_next / norm_now
    square = norm_next + 2.0 * ratio * cross + ratio * ratio * norm_now
    curve = ridge * square + (sums[0:1] + 2.0 * ratio * sums[1:2] + ratio * ratio * sums[2:3])
    step = norm_next / curve
    r = b - alpha * c
    out[0] = alpha * b + step * (r + ratio * b)
    out[1] = r - step * ((c - alpha * d) + ratio * c)

    for phase in range(5):
        pltpu.make_async_copy(
            sent.at[phase, pl.ds(0, n_exp - 1)], got.at[phase, pl.ds(0, n_exp - 1)], sends.at[phase]).wait()
    for turn in range(3):
        pltpu.make_async_copy(
            shares.at[turn, pl.ds(0, 3)], shares.at[turn, pl.ds(0, 3)], sends.at[5 + turn]).wait()
    for turn in range(2):
        pltpu.make_async_copy(
            dots.at[turn, pl.ds(0, n_exp - 1)], dots.at[turn, pl.ds(0, n_exp - 1)], sends.at[8 + turn]).wait()


def body(obs_weight, magnitude, star_id, peer_count, zp_index):
    n_sky, n_exp = lax.axis_size("sky"), lax.axis_size("exp")
    blocks = (n_exp, SUB, LANES)
    owned = pltpu.VMEM((2, ZP_PAD, LANES), f32)
    anywhere = pl.BlockSpec(memory_space=pl.ANY)
    inside = pl.BlockSpec(memory_space=pltpu.VMEM)
    both = pl.pallas_call(
        functools.partial(kernel, n_sky, n_exp),
        out_shape=owned,
        in_specs=[pl.BlockSpec(memory_space=pltpu.SMEM)] + [anywhere] * 4,
        out_specs=inside,
        scratch_shapes=[
            pltpu.VMEM(blocks, f32),
            pltpu.VMEM(blocks, f32),
            pltpu.VMEM(blocks, jnp.int32),
            pltpu.VMEM(blocks, jnp.int32),
            pltpu.VMEM((STAR_ROWS, LANES), f32),
            pltpu.VMEM((STAR_ROWS, LANES), f32),
            pltpu.VMEM((3, ZP_PAD, LANES), f32),
            pltpu.VMEM((SUB, LANES), f32),
            pltpu.VMEM((5,) + blocks, f32),
            pltpu.VMEM((5,) + blocks, f32),
            pltpu.VMEM((3, n_sky, ZP_PAD + SUB, LANES), f32),
            pltpu.VMEM((2, n_exp, SUB, LANES), f32),
            pltpu.SemaphoreType.DMA((4, SUB)),
            pltpu.SemaphoreType.DMA((10,)),
            pltpu.SemaphoreType.DMA((10, CHIPS // 4)),
        ],
        compiler_params=pltpu.CompilerParams(collective_id=0, has_side_effects=True),
        name="ubercal_cg",
    )(peer_count, obs_weight, magnitude, star_id, zp_index)
    return both[0].reshape(-1)[:ZP_DEV], both[1].reshape(-1)[:ZP_DEV]


def solution(mesh):
    return jax.shard_map(
        body,
        mesh=mesh,
        in_specs=(
            P("sky", "exp", None, None),
            P("sky", "exp", None, None),
            P("sky", "exp", None, None),
            P("sky", "exp", None),
            P("sky", "exp", None, None),
        ),
        out_specs=(P("exp"), P("exp")),
        check_vma=False,
    )
```

```python
import functools

import jax
import jax.numpy as jnp
from jax import lax
from jax.experimental import pallas as pl
from jax.experimental.pallas import tpu as pltpu
from jax.sharding import PartitionSpec as P

CAP = 1024
STAR_DEV = 4096
ZP_DEV = 12096
LANES = 128
SUB = CAP // LANES
STAR_ROWS = STAR_DEV // LANES
ZP_ROWS = (ZP_DEV + LANES - 1) // LANES
ZP_PAD = 96
PLANE = 8

OFFSETS = ((0, 0), (0, 1), (0, 3), (1, 0), (3, 0), (1, 1), (0, 2), (2, 0),
           (1, 3), (3, 1), (3, 3), (2, 1), (2, 2), (2, 3), (1, 2), (3, 2))
CHIPS = len(OFFSETS)


def digits(values):
    code = sum(v << (2 * q) for q, v in enumerate(values))
    return code - (1 << 32) if code >= 1 << 31 else code


OFFSET_Z = digits([z for z, _ in OFFSETS])
OFFSET_Y = digits([y for _, y in OFFSETS])

ridge = 1.0
prior = 1.0
f32 = jnp.float32
bf16 = jnp.bfloat16
NT = (((1,), (1,)), ((), ()))
MESH = pl.DeviceIdType.MESH


def two_parts(x):
    coarse = x.astype(bf16)
    return coarse, (x - coarse.astype(f32)).astype(bf16)


def as_code(x):
    return x.astype(f32).astype(bf16)


def row_of(x, r, n):
    return jnp.broadcast_to(x[r : r + 1, :], (n, LANES))


def scatter(high, low, parts, n_high, n_low):
    rows = high.shape[0]
    iota_high = as_code(lax.broadcasted_iota(jnp.int32, (n_high, LANES), 0))
    iota_low = as_code(lax.broadcasted_iota(jnp.int32, (n_low, LANES), 0))
    one, zero = jnp.ones((), bf16), jnp.zeros((), bf16)
    hot, weighted = [], [[] for _ in parts]
    for r in range(rows):
        hot.append(jnp.where(row_of(high, r, n_high) == iota_high, one, zero))
        mask = row_of(low, r, n_low) == iota_low
        for column, part in zip(weighted, parts):
            column.append(jnp.where(mask, row_of(part, r, n_low), zero))
    hot = jnp.concatenate(hot, axis=1)
    weighted = jnp.concatenate([jnp.concatenate(c, axis=1) for c in weighted], axis=0)
    return lax.dot_general(hot, weighted, NT, preferred_element_type=f32)


def pick(table, rows, index):
    high, low = lax.shift_right_logical(index, 7), index & 127
    found = jnp.zeros(index.shape, f32)
    for r in range(rows):
        line = jnp.broadcast_to(table[r : r + 1, :], index.shape)
        found = jnp.where(high == r, jnp.take_along_axis(line, low, axis=1), found)
    return found


def star_codes(index):
    high = lax.shift_right_logical(index, 7) + STAR_ROWS * (lax.shift_right_logical(index, 5) & 3)
    return as_code(high), as_code(index & 31)


def zp_codes(index):
    high = lax.shift_right_logical(index, 7) + ZP_PAD * (lax.shift_right_logical(index, 6) & 1)
    return as_code(high), as_code(index & 63)


def star_table(pair):
    both = pair[:, :32] + pair[:, 32:64]
    return jnp.concatenate([both[32 * q : 32 * q + 32, :] for q in range(4)], axis=1)


def kernel(
    n_sky, n_exp,
    count, weight_in, magnitude_in, star_in, zp_in,
    out,
    weight, magnitude, star, zp, wsum, mean, fields, scale,
    sent, got, shares, dots, loads, sends, arrivals,
):
    sky, me = lax.axis_index("sky"), lax.axis_index("exp")
    my_z, my_y, my_c = me // 8, (me // 2) % 4, me % 2
    partner = 1 - my_c

    def digit(code, q):
        return lax.shift_right_logical(jnp.int32(code), 2 * q) & 3

    def member(q, sign):
        z = (my_z + 4 + sign * digit(OFFSET_Z, q)) & 3
        y = (my_y + 4 + sign * digit(OFFSET_Y, q)) & 3
        return z * 8 + y * 2

    incoming = []
    for a, (source, target) in enumerate(((weight_in, weight), (star_in, star), (magnitude_in, magnitude), (zp_in, zp))):
        for c in range(SUB):
            copy = pltpu.make_async_copy(
                source.at[0, 0, :, pl.ds(c * LANES, LANES)], target.at[:, c, :], loads.at[a, c])
            copy.start()
            incoming.append(copy)

    barrier = pltpu.get_barrier_semaphore()

    @pl.loop(1, n_exp)
    def _(t):
        pl.semaphore_signal(barrier, inc=1, device_id={"exp": lax.rem(me + t, n_exp)}, device_id_type=MESH)

    for t in range(1, n_sky):
        pl.semaphore_signal(barrier, inc=1, device_id={"sky": lax.rem(sky + t, n_sky)}, device_id_type=MESH)

    for copy in incoming[: 3 * SUB]:
        copy.wait()

    slot = lax.broadcasted_iota(jnp.int32, (SUB, LANES), 0) * LANES + lax.broadcasted_iota(jnp.int32, (SUB, LANES), 1)

    def stack(blocks):
        return jnp.concatenate(blocks, axis=0)

    def first(g, total):
        base = g * (2 * PLANE)
        live = []
        for i in range(2 * PLANE):
            live.append(jnp.where(slot < count[0, 0, base + i], weight[base + i], 0.0))
            weight[base + i] = live[i]
        w = stack(live)
        high, low = star_codes(stack([star[base + i] for i in range(2 * PLANE)]))
        value = w * stack([magnitude[base + i] for i in range(2 * PLANE)])
        return total + scatter(high, low, two_parts(w) + two_parts(value), 128, 32)

    total = lax.fori_loop(0, n_exp // (2 * PLANE), first, jnp.zeros((128, 128), f32))
    wsum[...] = prior + star_table(total[:, :64])
    mean[...] = star_table(total[:, 64:]) / wsum[...]

    pl.semaphore_wait(barrier, n_exp - 1 + n_sky - 1)

    def exchange(phase, block, turned):
        @pl.loop(0, CHIPS // 2)
        def _(pair):
            todo = []
            for u in range(2):
                q = CHIPS - 1 - 2 * pair - u if turned else 2 * pair + u
                base = member(q, 1)
                for core in (partner, my_c):
                    j = base + core
                    todo.append((j, q, core is my_c and u == (1 if turned else 0)))
            made = [block(j) for j, _, _ in todo]
            for (j, _, _), x in zip(todo, made):
                sent[phase, j] = x
            for j, q, maybe_own in todo:
                def send(j=j, q=q):
                    pltpu.make_async_remote_copy(
                        src_ref=sent.at[phase, j], dst_ref=got.at[phase, me],
                        send_sem=sends.at[phase], recv_sem=arrivals.at[phase, q // 4],
                        device_id={"exp": j}, device_id_type=MESH).start()

                if maybe_own:
                    pl.when(q != 0)(send)

                    @pl.when(q == 0)
                    def _():
                        pltpu.make_async_copy(sent.at[phase, me], got.at[phase, me], arrivals.at[phase, 0]).start()
                else:
                    send()

    def arrive(phase, group):
        pltpu.make_async_copy(
            sent.at[phase, pl.ds(0, PLANE)], got.at[phase, pl.ds(0, PLANE)], arrivals.at[phase, group]).wait()

    def over_groups(phase, shape, turned, part):
        def one(step, total):
            group = CHIPS // 4 - 1 - step if turned else step
            js = []
            for u in range(4):
                base = member(4 * group + u, -1)
                js += [base, base + 1]
            arrive(phase, group)
            return total + part(js)

        return lax.fori_loop(0, CHIPS // 4, one, jnp.zeros(shape, f32))

    def to_owners(phase, values):
        exchange(phase, lambda j: weight[j] * (values(j) - pick(mean, STAR_ROWS, star[j])), False)

    def star_means(phase):
        def part(js):
            high, low = star_codes(stack([star[j] for j in js]))
            value = stack([weight[j] for j in js]) * stack([got[phase, j] for j in js])
            return scatter(high, low, two_parts(value), 128, 32)

        mean[...] = star_table(over_groups(phase, (128, 64), True, part)) / wsum[...]

    def owner_sums(phase, turn, before_sending=lambda: None):
        def part(js):
            high, low = zp_codes(stack([zp[j] for j in js]))
            return scatter(high, low, two_parts(stack([got[phase, j] for j in js])), 2 * ZP_PAD, 64)

        total = over_groups(phase, (2 * ZP_PAD, LANES), False, part)
        both = total + pltpu.roll(total, 64, 1)
        lane = lax.broadcasted_iota(jnp.int32, (ZP_PAD, LANES), 1)
        shares[turn, sky] = jnp.where(lane < 64, both[:ZP_PAD], both[ZP_PAD:])
        before_sending()
        for t in (2, 1, 3):
            pltpu.make_async_remote_copy(
                src_ref=shares.at[turn, sky], dst_ref=shares.at[turn, sky],
                send_sem=sends.at[5 + turn], recv_sem=arrivals.at[5 + turn, 0],
                device_id={"sky": lax.rem(sky + t, n_sky)}, device_id_type=MESH).start()
        pltpu.make_async_copy(
            shares.at[turn, pl.ds(0, 3)], shares.at[turn, pl.ds(0, 3)], arrivals.at[5 + turn, 0]).wait()
        part = [shares[turn, i] for i in range(4)]
        return (part[0] + part[1]) + (part[2] + part[3])

    def put_dots(turn, rows):
        dots[turn, me] = stack(rows + [jnp.zeros((1, LANES), f32)] * (SUB - len(rows)))

        @pl.loop(1, n_exp)
        def _(t):
            pltpu.make_async_remote_copy(
                src_ref=dots.at[turn, me], dst_ref=dots.at[turn, me],
                send_sem=sends.at[8 + turn], recv_sem=arrivals.at[8 + turn, 0],
                device_id={"exp": lax.rem(me + t, n_exp)}, device_id_type=MESH).start()

    def take_dots(turn):
        pltpu.make_async_copy(
            dots.at[turn, pl.ds(0, n_exp - 1)], dots.at[turn, pl.ds(0, n_exp - 1)], arrivals.at[8 + turn, 0]).wait()
        return jnp.sum(dots[turn], axis=0)

    def column(x):
        return jnp.sum(x, axis=0, keepdims=True)

    diagonal = (lax.broadcasted_iota(jnp.int32, (SUB, LANES), 0)
                == lax.broadcasted_iota(jnp.int32, (SUB, LANES), 1))

    to_owners(0, lambda j: magnitude[j])
    for copy in incoming[3 * SUB :]:
        copy.wait()
    fields[0] = owner_sums(0, 0)

    @pl.loop(0, 2)
    def _(turn):
        taken, given = 2 * turn + 1, 2 * turn + 2
        exchange(taken, lambda k: pick(fields.at[turn], ZP_ROWS, zp[k]), True)

        @pl.when(turn == 1)
        def _():
            b, c = fields[0], fields[1]
            put_dots(0, [column(b * b), column(b * c)])

        star_means(taken)
        to_owners(given, lambda j: got[taken, j])

        @pl.when(turn == 1)
        def _():
            sums = jnp.sum(take_dots(0), axis=1, keepdims=True)
            alpha = jnp.broadcast_to(sums[0:1] / sums[1:2], (1, LANES))
            scale[0:1] = alpha
            scale[1:2] = jnp.broadcast_to(sums[0:1], (1, LANES))
            b, c = fields[0], fields[1]
            r = b - alpha * c
            slots = [jnp.zeros((SUB, LANES), f32)] * 3

            def add(j, slots):
                v, t = got[1, j], sent[2, j]
                w, s = v - alpha * got[3, j], t - alpha * sent[4, j]
                return [slots[0] + w * s, slots[1] + v * s, slots[2] + v * t]

            slots = lax.fori_loop(0, n_exp, add, slots, unroll=4)
            put_dots(1, [column(x) for x in slots] + [column(r * r), column(r * b)])

        def with_dots():
            @pl.when(turn == 1)
            def _():
                sums = jnp.sum(take_dots(1), axis=1, keepdims=True)
                shares[2, sky, pl.ds(ZP_PAD - 1, 1)] = column(jnp.where(diagonal, sums, 0.0))

        fields[turn + 1] = owner_sums(given, turn + 1, with_dots) + ridge * fields[turn]

    b, c, d = fields[0], fields[1], fields[2]
    alpha, norm_now = scale[0:1], scale[1:2]
    sums = jnp.sum(jnp.where(diagonal, d[ZP_PAD - 1 :], 0.0), axis=1, keepdims=True)
    sums = jnp.broadcast_to(sums, (SUB, LANES))
    norm_next, cross = 0.25 * sums[3:4], 0.25 * sums[4:5]
    ratio = norm_next / norm_now
    square = norm_next + 2.0 * ratio * cross + ratio * ratio * norm_now
    curve = ridge * square + (sums[0:1] + 2.0 * ratio * sums[1:2] + ratio * ratio * sums[2:3])
    step = norm_next / curve
    r = b - alpha * c
    out[0] = alpha * b + step * (r + ratio * b)
    out[1] = r - step * ((c - alpha * d) + ratio * c)

    for phase in range(5):
        pltpu.make_async_copy(
            sent.at[phase, pl.ds(0, n_exp - 1)], got.at[phase, pl.ds(0, n_exp - 1)], sends.at[phase]).wait()
    for turn in range(3):
        pltpu.make_async_copy(
            shares.at[turn, pl.ds(0, 3)], shares.at[turn, pl.ds(0, 3)], sends.at[5 + turn]).wait()
    for turn in range(2):
        pltpu.make_async_copy(
            dots.at[turn, pl.ds(0, n_exp - 1)], dots.at[turn, pl.ds(0, n_exp - 1)], sends.at[8 + turn]).wait()


def body(obs_weight, magnitude, star_id, peer_count, zp_index):
    n_sky, n_exp = lax.axis_size("sky"), lax.axis_size("exp")
    blocks = (n_exp, SUB, LANES)
    owned = pltpu.VMEM((2, ZP_PAD, LANES), f32)
    anywhere = pl.BlockSpec(memory_space=pl.ANY)
    inside = pl.BlockSpec(memory_space=pltpu.VMEM)
    both = pl.pallas_call(
        functools.partial(kernel, n_sky, n_exp),
        out_shape=owned,
        in_specs=[pl.BlockSpec(memory_space=pltpu.SMEM)] + [anywhere] * 4,
        out_specs=inside,
        scratch_shapes=[
            pltpu.VMEM(blocks, f32),
            pltpu.VMEM(blocks, f32),
            pltpu.VMEM(blocks, jnp.int32),
            pltpu.VMEM(blocks, jnp.int32),
            pltpu.VMEM((STAR_ROWS, LANES), f32),
            pltpu.VMEM((STAR_ROWS, LANES), f32),
            pltpu.VMEM((3, ZP_PAD, LANES), f32),
            pltpu.VMEM((SUB, LANES), f32),
            pltpu.VMEM((5,) + blocks, f32),
            pltpu.VMEM((5,) + blocks, f32),
            pltpu.VMEM((3, n_sky, ZP_PAD, LANES), f32),
            pltpu.VMEM((2, n_exp, SUB, LANES), f32),
            pltpu.SemaphoreType.DMA((4, SUB)),
            pltpu.SemaphoreType.DMA((10,)),
            pltpu.SemaphoreType.DMA((10, CHIPS // 4)),
        ],
        compiler_params=pltpu.CompilerParams(collective_id=0, has_side_effects=True),
        name="ubercal_cg",
    )(peer_count, obs_weight, magnitude, star_id, zp_index)
    return both[0].reshape(-1)[:ZP_DEV], both[1].reshape(-1)[:ZP_DEV]


def solution(mesh):
    return jax.shard_map(
        body,
        mesh=mesh,
        in_specs=(
            P("sky", "exp", None, None),
            P("sky", "exp", None, None),
            P("sky", "exp", None, None),
            P("sky", "exp", None),
            P("sky", "exp", None, None),
        ),
        out_specs=(P("exp"), P("exp")),
        check_vma=False,
    )
```

```python
import functools

import jax
import jax.numpy as jnp
from jax import lax
from jax.experimental import pallas as pl
from jax.experimental.pallas import tpu as pltpu
from jax.sharding import PartitionSpec as P

CAP = 1024
STAR_DEV = 4096
ZP_DEV = 12096
LANES = 128
SUB = CAP // LANES
STAR_ROWS = STAR_DEV // LANES
ZP_ROWS = (ZP_DEV + LANES - 1) // LANES
ZP_PAD = 96
PLANE = 8

OFFSETS = ((0, 0), (0, 1), (0, 3), (1, 0), (3, 0), (1, 1), (0, 2), (2, 0),
           (1, 3), (3, 1), (3, 3), (2, 1), (2, 2), (2, 3), (1, 2), (3, 2))
CHIPS = len(OFFSETS)


def digits(values):
    code = sum(v << (2 * q) for q, v in enumerate(values))
    return code - (1 << 32) if code >= 1 << 31 else code


OFFSET_Z = digits([z for z, _ in OFFSETS])
OFFSET_Y = digits([y for _, y in OFFSETS])

ridge = 1.0
prior = 1.0
f32 = jnp.float32
bf16 = jnp.bfloat16
NT = (((1,), (1,)), ((), ()))
MESH = pl.DeviceIdType.MESH


def two_parts(x):
    coarse = x.astype(bf16)
    return coarse, (x - coarse.astype(f32)).astype(bf16)


def as_code(x):
    return x.astype(f32).astype(bf16)


def row_of(x, r, n):
    return jnp.broadcast_to(x[r : r + 1, :], (n, LANES))


def scatter(high, low, parts, n_high, n_low):
    rows = high.shape[0]
    iota_high = as_code(lax.broadcasted_iota(jnp.int32, (n_high, LANES), 0))
    iota_low = as_code(lax.broadcasted_iota(jnp.int32, (n_low, LANES), 0))
    one, zero = jnp.ones((), bf16), jnp.zeros((), bf16)
    hot, weighted = [], [[] for _ in parts]
    for r in range(rows):
        hot.append(jnp.where(row_of(high, r, n_high) == iota_high, one, zero))
        mask = row_of(low, r, n_low) == iota_low
        for column, part in zip(weighted, parts):
            column.append(jnp.where(mask, row_of(part, r, n_low), zero))
    hot = jnp.concatenate(hot, axis=1)
    weighted = jnp.concatenate([jnp.concatenate(c, axis=1) for c in weighted], axis=0)
    return lax.dot_general(hot, weighted, NT, preferred_element_type=f32)


def pick(table, rows, index):
    high, low = lax.shift_right_logical(index, 7), index & 127
    found = jnp.zeros(index.shape, f32)
    for r in range(rows):
        line = jnp.broadcast_to(table[r : r + 1, :], index.shape)
        found = jnp.where(high == r, jnp.take_along_axis(line, low, axis=1), found)
    return found


def star_codes(index):
    high = lax.shift_right_logical(index, 7) + STAR_ROWS * (lax.shift_right_logical(index, 5) & 3)
    return as_code(high), as_code(index & 31)


def zp_codes(index):
    high = lax.shift_right_logical(index, 7) + ZP_PAD * (lax.shift_right_logical(index, 6) & 1)
    return as_code(high), as_code(index & 63)


def star_table(pair):
    both = pair[:, :32] + pair[:, 32:64]
    return jnp.concatenate([both[32 * q : 32 * q + 32, :] for q in range(4)], axis=1)


def kernel(
    n_sky, n_exp,
    count, weight_in, magnitude_in, star_in, zp_in,
    out,
    weight, magnitude, star, zp, wsum, mean, fields, scale,
    sent, got, shares, dots, loads, sends, arrivals,
):
    sky, me = lax.axis_index("sky"), lax.axis_index("exp")
    my_z, my_y, my_c = me // 8, (me // 2) % 4, me % 2
    partner = 1 - my_c

    def digit(code, q):
        return lax.shift_right_logical(jnp.int32(code), 2 * q) & 3

    def member(q, sign):
        z = (my_z + 4 + sign * digit(OFFSET_Z, q)) & 3
        y = (my_y + 4 + sign * digit(OFFSET_Y, q)) & 3
        return z * 8 + y * 2

    incoming = []
    for a, (source, target) in enumerate(((weight_in, weight), (star_in, star), (magnitude_in, magnitude), (zp_in, zp))):
        for c in range(SUB):
            copy = pltpu.make_async_copy(
                source.at[0, 0, :, pl.ds(c * LANES, LANES)], target.at[:, c, :], loads.at[a, c])
            copy.start()
            incoming.append(copy)

    barrier = pltpu.get_barrier_semaphore()

    @pl.loop(1, n_exp)
    def _(t):
        pl.semaphore_signal(barrier, inc=1, device_id={"exp": lax.rem(me + t, n_exp)}, device_id_type=MESH)

    for t in range(1, n_sky):
        pl.semaphore_signal(barrier, inc=1, device_id={"sky": lax.rem(sky + t, n_sky)}, device_id_type=MESH)

    for copy in incoming[: 3 * SUB]:
        copy.wait()

    slot = lax.broadcasted_iota(jnp.int32, (SUB, LANES), 0) * LANES + lax.broadcasted_iota(jnp.int32, (SUB, LANES), 1)

    def stack(blocks):
        return jnp.concatenate(blocks, axis=0)

    def first(g, total):
        base = g * (2 * PLANE)
        live = []
        for i in range(2 * PLANE):
            live.append(jnp.where(slot < count[0, 0, base + i], weight[base + i], 0.0))
            weight[base + i] = live[i]
        w = stack(live)
        high, low = star_codes(stack([star[base + i] for i in range(2 * PLANE)]))
        value = w * stack([magnitude[base + i] for i in range(2 * PLANE)])
        return total + scatter(high, low, two_parts(w) + two_parts(value), 128, 32)

    total = lax.fori_loop(0, n_exp // (2 * PLANE), first, jnp.zeros((128, 128), f32))
    wsum[...] = prior + star_table(total[:, :64])
    mean[...] = star_table(total[:, 64:]) / wsum[...]

    pl.semaphore_wait(barrier, n_exp - 1 + n_sky - 1)

    def exchange(phase, block, turned):
        @pl.loop(0, CHIPS // 2)
        def _(pair):
            todo = []
            for u in range(2):
                q = CHIPS - 1 - 2 * pair - u if turned else 2 * pair + u
                base = member(q, 1)
                for core in (partner, my_c):
                    j = base + core
                    todo.append((j, q, core is my_c and u == (1 if turned else 0)))
            made = [block(j) for j, _, _ in todo]
            for (j, _, _), x in zip(todo, made):
                sent[phase, j] = x
            for j, q, maybe_own in todo:
                def send(j=j, q=q):
                    pltpu.make_async_remote_copy(
                        src_ref=sent.at[phase, j], dst_ref=got.at[phase, me],
                        send_sem=sends.at[phase], recv_sem=arrivals.at[phase, q // 4],
                        device_id={"exp": j}, device_id_type=MESH).start()

                if maybe_own:
                    pl.when(q != 0)(send)

                    @pl.when(q == 0)
                    def _():
                        pltpu.make_async_copy(sent.at[phase, me], got.at[phase, me], arrivals.at[phase, 0]).start()
                else:
                    send()

    def arrive(phase, group):
        pltpu.make_async_copy(
            sent.at[phase, pl.ds(0, PLANE)], got.at[phase, pl.ds(0, PLANE)], arrivals.at[phase, group]).wait()

    def over_groups(phase, shape, turned, part):
        def one(step, total):
            group = CHIPS // 4 - 1 - step if turned else step
            js = []
            for u in range(4):
                base = member(4 * group + u, -1)
                js += [base, base + 1]
            arrive(phase, group)
            return total + part(js)

        return lax.fori_loop(0, CHIPS // 4, one, jnp.zeros(shape, f32))

    def to_owners(phase, values):
        exchange(phase, lambda j: weight[j] * (values(j) - pick(mean, STAR_ROWS, star[j])), False)

    def star_means(phase):
        def part(js):
            high, low = star_codes(stack([star[j] for j in js]))
            value = stack([weight[j] for j in js]) * stack([got[phase, j] for j in js])
            return scatter(high, low, two_parts(value), 128, 32)

        mean[...] = star_table(over_groups(phase, (128, 64), True, part)) / wsum[...]

    def owner_sums(phase, turn, before_sending=lambda: None):
        def part(js):
            high, low = zp_codes(stack([zp[j] for j in js]))
            return scatter(high, low, two_parts(stack([got[phase, j] for j in js])), 2 * ZP_PAD, 64)

        total = over_groups(phase, (2 * ZP_PAD, LANES), False, part)
        both = total + pltpu.roll(total, 64, 1)
        lane = lax.broadcasted_iota(jnp.int32, (ZP_PAD, LANES), 1)
        shares[turn, sky] = jnp.where(lane < 64, both[:ZP_PAD], both[ZP_PAD:])
        before_sending()
        for t in (2, 1, 3):
            pltpu.make_async_remote_copy(
                src_ref=shares.at[turn, sky], dst_ref=shares.at[turn, sky],
                send_sem=sends.at[5 + turn], recv_sem=arrivals.at[5 + turn, 0],
                device_id={"sky": lax.rem(sky + t, n_sky)}, device_id_type=MESH).start()
        pltpu.make_async_copy(
            shares.at[turn, pl.ds(0, 3)], shares.at[turn, pl.ds(0, 3)], arrivals.at[5 + turn, 0]).wait()
        part = [shares[turn, i] for i in range(4)]
        return (part[0] + part[1]) + (part[2] + part[3])

    sizes = (2, SUB)

    def put_dots(turn, rows):
        dots[turn, me] = stack(rows + [jnp.zeros((1, LANES), f32)] * (SUB - len(rows)))

        @pl.loop(1, n_exp)
        def _(t):
            pltpu.make_async_remote_copy(
                src_ref=dots.at[turn, me, pl.ds(0, sizes[turn])], dst_ref=dots.at[turn, me, pl.ds(0, sizes[turn])],
                send_sem=sends.at[8 + turn], recv_sem=arrivals.at[8 + turn, 0],
                device_id={"exp": lax.rem(me + t, n_exp)}, device_id_type=MESH).start()

    def take_dots(turn):
        pltpu.make_async_copy(
            dots.at[turn, pl.ds(0, n_exp - 1), pl.ds(0, sizes[turn])], dots.at[turn, pl.ds(0, n_exp - 1), pl.ds(0, sizes[turn])], arrivals.at[8 + turn, 0]).wait()
        return jnp.sum(dots[turn, :, pl.ds(0, sizes[turn])], axis=0)

    def column(x):
        return jnp.sum(x, axis=0, keepdims=True)

    diagonal = (lax.broadcasted_iota(jnp.int32, (SUB, LANES), 0)
                == lax.broadcasted_iota(jnp.int32, (SUB, LANES), 1))

    to_owners(0, lambda j: magnitude[j])
    for copy in incoming[3 * SUB :]:
        copy.wait()
    fields[0] = owner_sums(0, 0)

    @pl.loop(0, 2)
    def _(turn):
        taken, given = 2 * turn + 1, 2 * turn + 2
        exchange(taken, lambda k: pick(fields.at[turn], ZP_ROWS, zp[k]), True)

        @pl.when(turn == 1)
        def _():
            b, c = fields[0], fields[1]
            put_dots(0, [column(b * b), column(b * c)])

        star_means(taken)
        to_owners(given, lambda j: got[taken, j])

        @pl.when(turn == 1)
        def _():
            sums = jnp.sum(take_dots(0), axis=1, keepdims=True)
            alpha = jnp.broadcast_to(sums[0:1] / sums[1:2], (1, LANES))
            scale[0:1] = alpha
            scale[1:2] = jnp.broadcast_to(sums[0:1], (1, LANES))
            b, c = fields[0], fields[1]
            r = b - alpha * c
            slots = [jnp.zeros((SUB, LANES), f32)] * 3

            def add(j, slots):
                v, t = got[1, j], sent[2, j]
                w, s = v - alpha * got[3, j], t - alpha * sent[4, j]
                return [slots[0] + w * s, slots[1] + v * s, slots[2] + v * t]

            slots = lax.fori_loop(0, n_exp, add, slots, unroll=4)
            put_dots(1, [column(x) for x in slots] + [column(r * r), column(r * b)])

        def with_dots():
            @pl.when(turn == 1)
            def _():
                sums = jnp.sum(take_dots(1), axis=1, keepdims=True)
                shares[2, sky, pl.ds(ZP_PAD - 1, 1)] = column(jnp.where(diagonal, sums, 0.0))

        fields[turn + 1] = owner_sums(given, turn + 1, with_dots) + ridge * fields[turn]

    b, c, d = fields[0], fields[1], fields[2]
    alpha, norm_now = scale[0:1], scale[1:2]
    sums = jnp.sum(jnp.where(diagonal, d[ZP_PAD - 1 :], 0.0), axis=1, keepdims=True)
    sums = jnp.broadcast_to(sums, (SUB, LANES))
    norm_next, cross = 0.25 * sums[3:4], 0.25 * sums[4:5]
    ratio = norm_next / norm_now
    square = norm_next + 2.0 * ratio * cross + ratio * ratio * norm_now
    curve = ridge * square + (sums[0:1] + 2.0 * ratio * sums[1:2] + ratio * ratio * sums[2:3])
    step = norm_next / curve
    r = b - alpha * c
    out[0] = alpha * b + step * (r + ratio * b)
    out[1] = r - step * ((c - alpha * d) + ratio * c)

    for phase in range(5):
        pltpu.make_async_copy(
            sent.at[phase, pl.ds(0, n_exp - 1)], got.at[phase, pl.ds(0, n_exp - 1)], sends.at[phase]).wait()
    for turn in range(3):
        pltpu.make_async_copy(
            shares.at[turn, pl.ds(0, 3)], shares.at[turn, pl.ds(0, 3)], sends.at[5 + turn]).wait()
    for turn in range(2):
        pltpu.make_async_copy(
            dots.at[turn, pl.ds(0, n_exp - 1), pl.ds(0, sizes[turn])], dots.at[turn, pl.ds(0, n_exp - 1), pl.ds(0, sizes[turn])], sends.at[8 + turn]).wait()


def body(obs_weight, magnitude, star_id, peer_count, zp_index):
    n_sky, n_exp = lax.axis_size("sky"), lax.axis_size("exp")
    blocks = (n_exp, SUB, LANES)
    owned = pltpu.VMEM((2, ZP_PAD, LANES), f32)
    anywhere = pl.BlockSpec(memory_space=pl.ANY)
    inside = pl.BlockSpec(memory_space=pltpu.VMEM)
    both = pl.pallas_call(
        functools.partial(kernel, n_sky, n_exp),
        out_shape=owned,
        in_specs=[pl.BlockSpec(memory_space=pltpu.SMEM)] + [anywhere] * 4,
        out_specs=inside,
        scratch_shapes=[
            pltpu.VMEM(blocks, f32),
            pltpu.VMEM(blocks, f32),
            pltpu.VMEM(blocks, jnp.int32),
            pltpu.VMEM(blocks, jnp.int32),
            pltpu.VMEM((STAR_ROWS, LANES), f32),
            pltpu.VMEM((STAR_ROWS, LANES), f32),
            pltpu.VMEM((3, ZP_PAD, LANES), f32),
            pltpu.VMEM((SUB, LANES), f32),
            pltpu.VMEM((5,) + blocks, f32),
            pltpu.VMEM((5,) + blocks, f32),
            pltpu.VMEM((3, n_sky, ZP_PAD, LANES), f32),
            pltpu.VMEM((2, n_exp, SUB, LANES), f32),
            pltpu.SemaphoreType.DMA((4, SUB)),
            pltpu.SemaphoreType.DMA((10,)),
            pltpu.SemaphoreType.DMA((10, CHIPS // 4)),
        ],
        compiler_params=pltpu.CompilerParams(collective_id=0, has_side_effects=True),
        name="ubercal_cg",
    )(peer_count, obs_weight, magnitude, star_id, zp_index)
    return both[0].reshape(-1)[:ZP_DEV], both[1].reshape(-1)[:ZP_DEV]


def solution(mesh):
    return jax.shard_map(
        body,
        mesh=mesh,
        in_specs=(
            P("sky", "exp", None, None),
            P("sky", "exp", None, None),
            P("sky", "exp", None, None),
            P("sky", "exp", None),
            P("sky", "exp", None, None),
        ),
        out_specs=(P("exp"), P("exp")),
        check_vma=False,
    )
```
